32 devices in a mesh: lat: 4 (over z), comp: 8 (over y, x, core).
Axes of the slice: x: 2, y: 2, z: 4, core: 2. Of those that a mesh axis runs over, the one named last changes fastest.
Arguments:
- spectrum: float32 [1152, 64, 512], P('comp', 'lat'), may hold values from 0.05 to 2
- mask: int32 [64, 512], replicated, may hold values 0 or 1
- courant: float32 [2, 1152], P(None, 'comp'), may hold values from -0.5 to 0.5
- proj_a: bfloat16 [1152, 1152], P('comp'), may hold values from -0.1875 to 0.1875
- proj_b: bfloat16 [1152, 1152], P('comp'), may hold values from -0.1875 to 0.1875
- proj_c: bfloat16 [1152, 1152], P('comp'), may hold values from -0.1875 to 0.1875
- proj_d: bfloat16 [1152, 1152], P('comp'), may hold values from -0.1875 to 0.1875
- stokes_kernel: float32 [1152, 64], replicated, may hold values from -0.1875 to 0.1875
- tile_points: int32 [4, 8, 2048], P('lat', 'comp'), may hold values from 0 to 8191, as said below
- tile_counts: int32 [4, 8], P('lat', 'comp'), may hold values from 1 to 2048, as said below
- tile_nbr: int32 [4, 8, 2, 2048], P('lat', 'comp'), may hold values from 0 to 2047, as said below
- vorticity: float32 [4, 8, 64, 2048], P('lat', 'comp'), may hold values from -6 to 6
- diffusivity: float32 [4, 8, 64, 2048], P('lat', 'comp'), may hold values from 0.1 to 1
Outputs:
- spectrum_out: float32 [1152, 64, 512], P('comp', 'lat')
- ocean_force: float32 [4, 8, 64, 2048], P('lat', 'comp')
The draws below stay inside these ranges and needn't reach their ends.
Inputs may be any that keep to these rules, and one draw needn't show every extreme that they name: `mask`: 1 marks a sea cell, 0 land. `tile_points`: each entry is a point of the tile's own latitude group, numbered as in the reference program; the entries of one tile are distinct; of any block of 1024 point numbers starting at a multiple of 1024 a tile holds at most 512, and in every tile some block holds exactly 512; only the first tile_counts entries are live. `tile_counts`: in every latitude group some tile is full. `tile_nbr`: every entry is below its tile's count.
All inputs are finite; a program needn't handle non-finite values.
Results may differ from the reference program's by a relative error of at most 0.0033.
Values may be sent and summed in bfloat16 or wider, within the bound.
A program may use at most 128 MiB of HBM per device.

```python
import math
import jax
import jax.numpy as jnp
from jax import lax

K = 1152
L = 64
ADV = 2
NLON = 512
KC = 144
NR = 64
NPG = 8192
P_DEV = 1024
TILE_MOST = 2048
TILE_CAP = 512
N_LAT = 4
N_COMP = 8


def tile_layout(key):
    base = jax.random.fold_in(key, 4242)
    key_count, key_full, key_split, key_pair, key_pick, key_order, key_nbr, key_side = jax.random.split(base, 8)
    counts = jax.random.randint(key_count, (N_LAT, N_COMP), 1, TILE_MOST + 1)
    full_tile = jax.random.randint(key_full, (N_LAT,), 0, N_COMP)
    counts = jnp.where(jnp.arange(N_COMP)[None, :] == full_tile[:, None], TILE_MOST, counts).astype(jnp.int32)
    half_comp = N_COMP // 2
    first_share = jax.random.randint(key_split, (N_LAT, N_COMP, half_comp), 0, TILE_CAP + 1)
    forced_pair = jax.random.randint(key_pair, (N_LAT, N_COMP), 0, half_comp)
    forced_side = jax.random.randint(key_side, (N_LAT, N_COMP), 0, 2)
    forced_value = forced_side * TILE_CAP
    first_share = jnp.where(jnp.arange(half_comp)[None, None, :] == forced_pair[:, :, None], forced_value[:, :, None], first_share)
    shares = jnp.stack([first_share, TILE_CAP - first_share], axis=3).reshape(N_LAT, N_COMP, N_COMP)
    picks = jax.vmap(lambda single: jax.random.permutation(single, P_DEV))(jax.random.split(key_pick, N_LAT * N_COMP * N_COMP))
    picks = picks.reshape(N_LAT, N_COMP, N_COMP, P_DEV)[:, :, :, :TILE_CAP]
    owners = jnp.arange(N_COMP, dtype=jnp.int32)[None, None, :, None]
    candidates = (owners * P_DEV + picks).reshape(N_LAT, N_COMP, N_COMP * TILE_CAP)
    valid = (jnp.arange(TILE_CAP, dtype=jnp.int32)[None, None, None, :] < shares[:, :, :, None]).reshape(N_LAT, N_COMP, N_COMP * TILE_CAP)
    order = jnp.argsort(1 - valid.astype(jnp.int32), axis=2, stable=True)[:, :, :TILE_MOST]
    chosen = jnp.take_along_axis(candidates, order, axis=2)
    mixing = jax.vmap(lambda single: jax.random.permutation(single, TILE_MOST))(jax.random.split(key_order, N_LAT * N_COMP))
    mixing = mixing.reshape(N_LAT, N_COMP, TILE_MOST)
    points = jnp.take_along_axis(chosen, mixing, axis=2).astype(jnp.int32)
    shuffles = jax.vmap(lambda single: jax.random.permutation(single, TILE_MOST))(jax.random.split(key_nbr, N_LAT * N_COMP * 2))
    shuffles = shuffles.reshape(N_LAT, N_COMP, 2, TILE_MOST)
    neighbours = (shuffles % counts[:, :, None, None]).astype(jnp.int32)
    return (counts, points, neighbours)


def draw_tile_points(key, part):
    return tile_layout(key)[1]


def draw_tile_counts(key, part):
    return tile_layout(key)[0]


def draw_tile_nbr(key, part):
    return tile_layout(key)[2]


def set_ends(entries, stream_key, smallest, top_value):
    longest = entries.shape.index(max(entries.shape))
    spots = []
    for shift in (0, 1):
        where = [jax.random.randint(jax.random.fold_in(stream_key, axis), (), 0, length) for axis, length in enumerate(entries.shape)]
        where[longest] = (where[longest] + shift) % entries.shape[longest]
        spots.append(tuple(where))
    return entries.at[spots[0]].set(smallest).at[spots[1]].set(top_value)


def steps_of(own_key, dims, cuts, smallest, top_value):
    level = 1.0
    for position, blocks in cuts:
        steps = jax.random.uniform(jax.random.fold_in(jax.random.fold_in(own_key, 6), position), (blocks,), jnp.float32, smallest / len(cuts), top_value / len(cuts))
        level = level * jnp.repeat(jnp.exp(steps), dims[position] // blocks).reshape((-1,) + (1,) * (len(dims) - 1 - position))
    return level


def scatter_about(own_key, shape, width, limit, pieces=(), kind=jnp.bfloat16):
    array = width * jax.random.normal(own_key, shape, jnp.float32)
    if pieces:
        array = array * steps_of(own_key, shape, pieces, -0.22, 0.18)
    return jnp.clip(array, -limit, limit).astype(kind)


def setup_inputs(seed: int = 0) -> dict:
    splits = jax.random.split(jax.random.key(seed), 14)
    return {
        "spectrum": jnp.clip(jnp.exp(math.log(2.0) - 3.6888794 * jax.random.uniform(splits[0], (K, NR, NLON), jnp.float32) ** steps_of(splits[0], (K, NR, NLON), ((0, 8), (1, 4)), -0.2, 0.2)), 0.05, 2.0),
        "mask": set_ends((jax.random.randint(splits[1], (NR, NLON), 0, 4) < 3).astype(jnp.int32), jax.random.fold_in(splits[1], 1), 0, 1),
        "courant": jnp.clip(jax.random.uniform(splits[2], (2, K), jnp.float32, -0.5, 0.5) * steps_of(splits[2], (2, K), ((1, 8),), -0.4, 0.0), -0.5, 0.5),
        "proj_a": scatter_about(splits[3], (K, K), K ** -0.5, 0.1875, ((0, 8),)),
        "proj_b": scatter_about(splits[4], (K, K), K ** -0.5, 0.1875, ((0, 8),)),
        "proj_c": scatter_about(splits[5], (K, K), K ** -0.5, 0.1875, ((0, 8),)),
        "proj_d": scatter_about(splits[6], (K, K), K ** -0.5, 0.1875, ((0, 8),)),
        "stokes_kernel": scatter_about(splits[7], (K, L), K ** -0.5, 0.1875, (), jnp.float32),
        "tile_points": draw_tile_points(jax.random.fold_in(splits[13], 71), 0),
        "tile_counts": draw_tile_counts(jax.random.fold_in(splits[13], 71), 0),
        "tile_nbr": draw_tile_nbr(jax.random.fold_in(splits[13], 71), 0),
        "vorticity": scatter_about(splits[11], (N_LAT, N_COMP, L, TILE_MOST), 1.0, 6.0, ((0, 4), (1, 8)), jnp.float32),
        "diffusivity": jnp.clip(jnp.exp(math.log(1.0) - 2.3025851 * jax.random.uniform(splits[12], (N_LAT, N_COMP, L, TILE_MOST), jnp.float32) ** steps_of(splits[12], (N_LAT, N_COMP, L, TILE_MOST), ((0, 4), (1, 8)), -0.2, 0.2)), 0.1, 1.0),
    }


time_step = 0.25


def limiter(backward, forward):
    orient = jnp.sign(backward)
    bound = jnp.minimum(jnp.minimum(2.0 * jnp.abs(backward), orient * (backward + 2.0 * forward) / 3.0), 2.0 * orient * forward)
    return orient * jnp.maximum(bound, 0.0)


def face_flux(before, center, after, beyond, speed):
    plus_face = center + 0.5 * limiter(center - before, after - center)
    minus_face = after + 0.5 * limiter(after - beyond, center - after)
    return jnp.maximum(speed, 0.0) * plus_face + jnp.minimum(speed, 0.0) * minus_face


def lon_sweep(energy, speed, sea_part):
    flux = face_flux(jnp.roll(energy, 1, 2), energy, jnp.roll(energy, -1, 2), jnp.roll(energy, -2, 2), speed)
    return sea_part * (energy - (flux - jnp.roll(flux, 1, 2)))


def lat_sweep(padded, speed, sea_part):
    extent = padded.shape[1] - 4
    flux = face_flux(padded[:, 0:extent + 1], padded[:, 1:extent + 2], padded[:, 2:extent + 3], padded[:, 3:extent + 4], speed)
    return sea_part * (padded[:, 2:extent + 2] - (flux[:, 1:] - flux[:, :-1]))


def ocean_tile(profile, points, count, neighbours, vort_tile, diff_tile):
    slots = jnp.take(profile, points, axis=1).astype(jnp.float32)
    live = (jnp.arange(slots.shape[1], dtype=jnp.int32) < count).astype(jnp.float32)
    east = jnp.take(slots, neighbours[0], axis=1)
    north = jnp.take(slots, neighbours[1], axis=1)
    upper = jnp.concatenate([slots[:1], slots[:-1]], axis=0)
    lower = jnp.concatenate([slots[1:], jnp.zeros_like(slots[:1])], axis=0)
    return live[None, :] * (vort_tile * (east - north) + diff_tile * (upper - 2.0 * slots + lower))


def reference(spectrum, mask, courant, proj_a, proj_b, proj_c, proj_d, stokes_kernel, tile_points, tile_counts, tile_nbr, vorticity, diffusivity):
    sea_mask = mask.astype(jnp.float32)
    spectra_blocks = spectrum.reshape(N_COMP, KC, NR, NLON)
    speeds = courant.reshape(2, N_COMP, KC).transpose(1, 0, 2)

    def advect(operands):
        energy = operands[0] * sea_mask
        speed_lon = operands[1][0][:, None, None]
        speed_lat = operands[1][1][:, None, None]
        for substep in range(ADV):
            energy = lon_sweep(energy, speed_lon, sea_mask)
            padded = jnp.pad(energy, ((0, 0), (2, 2), (0, 0)))
            energy = lat_sweep(padded, speed_lat, sea_mask)
        return energy

    moved = lax.map(advect, (spectra_blocks, speeds)).reshape(K, NR, NLON)
    groups = moved.reshape(K, N_LAT, NPG).transpose(1, 0, 2)
    weight_a = proj_a.astype(jnp.float32)
    weight_b = proj_b.astype(jnp.float32)
    weight_c = proj_c.astype(jnp.float32)
    weight_d = proj_d.astype(jnp.float32)
    highest = lax.Precision.HIGHEST

    def source(band):
        first = jnp.dot(weight_a.T, band, precision=highest)
        second = jnp.dot(weight_b.T, band, precision=highest)
        product = first * second
        gain = jnp.dot(weight_c.T, product, precision=highest)
        loss = jnp.dot(weight_d.T, product, precision=highest)
        updated = band + time_step * (gain - band * loss)
        profile = jnp.dot(stokes_kernel.T, updated, precision=highest).astype(jnp.bfloat16)
        return updated, profile

    updated, profiles = lax.map(source, groups)
    spectrum_out = updated.transpose(1, 0, 2).reshape(K, NR, NLON)
    per_tile = jax.vmap(ocean_tile, in_axes=(None, 0, 0, 0, 0, 0))
    per_group = jax.vmap(per_tile, in_axes=(0, 0, 0, 0, 0, 0))
    ocean_force = per_group(profiles, tile_points, tile_counts, tile_nbr, vorticity, diffusivity)
    return spectrum_out, ocean_force
```

```python
import functools

import jax
import jax.numpy as jnp
from jax import lax
from jax.experimental import pallas as pl
from jax.experimental.pallas import tpu as pltpu
from jax.sharding import PartitionSpec as P

ADV = 2
time_step = 0.25
CB = 16
LANES = 128
LOW = 256
PIECES = 2


def half_limited(b, f):
    t = b * (1.0 / 6.0) + f * (1.0 / 3.0)
    low = jnp.minimum(jnp.maximum(b, f), 0.0)
    high = jnp.maximum(jnp.minimum(b, f), 0.0)
    return jnp.minimum(jnp.maximum(t, low), high)


def lane_blocks(ways):
    lane = lax.broadcasted_iota(jnp.int32, (8, LANES), 1)
    width = LANES // ways
    return lane, lane // width, lane % width


def spread(natural):
    ways = len(natural)
    _, block, at = lane_blocks(ways)
    picked = [
        jnp.take_along_axis(x, at * ways + (block + (ways - j)) % ways, axis=1)
        for j, x in enumerate(natural)
    ]
    out = []
    for v in range(ways):
        z = picked[-v % ways]
        for k in range(1, ways):
            z = jnp.where(block == k, picked[(k - v) % ways], z)
        out.append(pltpu.roll(z, LANES - v * (LANES // ways), 1) if v else z)
    return out


def gather_back(parts):
    ways = len(parts)
    lane, block, _ = lane_blocks(ways)
    width = LANES // ways
    turned = [pltpu.roll(x, v * width, 1) if v else x for v, x in enumerate(parts)]
    out = []
    for j in range(ways):
        y = turned[-j % ways]
        for k in range(1, ways):
            y = jnp.where(block == k, turned[(k - j) % ways], y)
        index = (lane % ways + j) % ways * width + lane // ways
        out.append(jnp.take_along_axis(y, index, axis=1))
    return out


def speeds(column):
    c = jnp.broadcast_to(column, (8, LANES))
    return c, jnp.abs(c), c > 0.0


def lon_row(e, sea, speed):
    c, a, pos = speed
    ways = len(e)
    nxt = e[1:] + [pltpu.roll(e[0], LANES - 1, 1)]
    d = [n - x for n, x in zip(nxt, e)]
    before = [pltpu.roll(d[-1], 1, 1)] + d[:-1]
    after = d[1:] + [pltpu.roll(d[0], LANES - 1, 1)]
    flux = [
        c * jnp.where(pos, e[v], nxt[v]) + a * half_limited(jnp.where(pos, before[v], after[v]), d[v])
        for v in range(ways)
    ]
    behind = [pltpu.roll(flux[-1], 1, 1)] + flux[:-1]
    return [sea[v] * (e[v] - (flux[v] - behind[v])) for v in range(ways)]


def parts_of(row):
    return [row[:, j * LANES : (j + 1) * LANES] for j in range(row.shape[1] // LANES)]


def first_kernel(rows, x_ref, mask_ref, cour_ref, out_ref, x_s):
    lon = x_ref.shape[1]
    ways = lon // LANES
    for t in range(x_ref.shape[0] // 8):
        tile = spread([x_ref[t * 8 : t * 8 + 8, j * LANES : (j + 1) * LANES] for j in range(ways)])
        for v in range(ways):
            x_s[v, t * 8 : t * 8 + 8, :] = tile[v]

    @pl.loop(0, CB // 8)
    def _(half):
        base = pl.multiple_of(half * 8, 8)
        speed = speeds(cour_ref[pl.ds(base, 8), 0:1])
        for r in range(rows):
            sea = parts_of(mask_ref[r : r + 1, :])
            e = [x_s[v, pl.ds(half * (8 * rows) + r, 8, stride=rows), :] * sea[v] for v in range(ways)]
            out = lon_row(e, sea, speed)
            for v in range(ways):
                out_ref[r, pl.ds(base, 8), v * LANES : (v + 1) * LANES] = out[v]


def first_sweep(spectrum, mask_rows, cour):
    comps, rows, lon = spectrum.shape
    return pl.pallas_call(
        functools.partial(first_kernel, rows),
        grid=(pl.cdiv(comps, CB),),
        in_specs=[
            pl.BlockSpec((CB * rows, lon), lambda i: (i, 0)),
            pl.BlockSpec((rows, lon), lambda i: (0, 0)),
            pl.BlockSpec((CB, 2), lambda i: (i, 0)),
        ],
        out_specs=pl.BlockSpec((rows, CB, lon), lambda i: (0, i, 0)),
        out_shape=jax.ShapeDtypeStruct((rows, comps, lon), jnp.float32),
        scratch_shapes=[pltpu.VMEM((lon // LANES, CB * rows, LANES), jnp.float32)],
        cost_estimate=pl.CostEstimate(
            flops=comps * rows * lon * 400, bytes_accessed=comps * rows * lon * 8, transcendentals=0
        ),
        name="first_sweep",
    )(spectrum.reshape(comps * rows, lon), mask_rows, cour)


def advect_kernel(rows, chunk, x_ref, up_ref, dn_ref, mask_ref, cour_ref, band_ref, a_s, b_s, u_s):
    lon = x_ref.shape[2]
    ways = lon // LANES
    margin = 2 * ADV
    total = rows + 2 * margin
    for r in range(margin):
        u_s[r] = up_ref[r].astype(jnp.float32)
        u_s[margin + r] = dn_ref[r].astype(jnp.float32)

    @pl.loop(0, CB // 8)
    def _(half):
        base = pl.multiple_of(half * 8, 8)
        cour = cour_ref[pl.ds(base, 8), :]
        lon_speed = speeds(cour[:, 0:1])
        c, a, pos = speeds(cour[:, 1:2])

        def sea_row(r):
            return parts_of(mask_ref[r : r + 1, :])

        def put(ref, r, value):
            for v in range(ways):
                ref[r, :, v * LANES : (v + 1) * LANES] = value[v]

        def swept_row(r):
            if margin <= r < margin + rows:
                return parts_of(x_ref[r - margin, pl.ds(base, 8), :])
            return parts_of(a_s[r])

        for k in range(2 * margin):
            r = k if k < margin else rows + k
            sea = sea_row(r)
            e = spread(parts_of(u_s[k, pl.ds(base, 8), :]))
            put(a_s, r, lon_row([e[v] * sea[v] for v in range(ways)], sea, lon_speed))

        for substep in range(ADV):
            gone = 2 * substep
            row = swept_row
            if substep:
                for r in range(gone, total - gone):
                    put(a_s, r, lon_row(parts_of(b_s[r]), sea_row(r), lon_speed))
                row = lambda r: parts_of(a_s[r])
            for v in range(ways):
                cur, nxt = row(gone)[v], row(gone + 1)[v]
                d, fl = nxt - cur, None
                ahead = row(gone + 2)[v]
                dp = ahead - nxt
                for r in range(gone + 1, total - gone - 2):
                    cur, nxt, dm, d = nxt, ahead, d, dp
                    ahead = row(r + 2)[v]
                    dp = ahead - nxt
                    now = c * jnp.where(pos, cur, nxt) + a * half_limited(jnp.where(pos, dm, dp), d)
                    if fl is not None:
                        value = sea_row(r)[v] * (cur - (now - fl))
                        if substep == ADV - 1:
                            at = (r - margin) * lon + v * LANES
                            to, lane = divmod(at, chunk)
                            band_ref[to, pl.ds(base, 8), lane : lane + LANES] = value
                        else:
                            b_s[r, :, v * LANES : (v + 1) * LANES] = value
                    fl = now


def advect(swept, halo_up, halo_dn, mask_rows, cour, dests, first, size):
    rows, comps, lon = swept.shape
    chunk = rows * lon // dests
    margin = 2 * ADV
    skip = first // CB
    total = rows + 2 * margin
    return pl.pallas_call(
        functools.partial(advect_kernel, rows, chunk),
        grid=(pl.cdiv(size, CB),),
        in_specs=[
            pl.BlockSpec((rows, CB, lon), lambda i: (0, i + skip, 0)),
            pl.BlockSpec((margin, CB, lon), lambda i: (0, i + skip, 0)),
            pl.BlockSpec((margin, CB, lon), lambda i: (0, i + skip, 0)),
            pl.BlockSpec((total, lon), lambda i: (0, 0)),
            pl.BlockSpec((CB, 2), lambda i: (i + skip, 0)),
        ],
        out_specs=pl.BlockSpec((dests, CB, chunk), lambda i: (0, i, 0)),
        out_shape=jax.ShapeDtypeStruct((dests, size, chunk), jnp.float32),
        scratch_shapes=[
            pltpu.VMEM((total, 8, lon), jnp.float32),
            pltpu.VMEM((total, 8, lon), jnp.float32),
            pltpu.VMEM((2 * margin, CB, lon), jnp.float32),
        ],
        cost_estimate=pl.CostEstimate(
            flops=size * rows * lon * 400, bytes_accessed=size * rows * lon * 8, transcendentals=0
        ),
        name="advect",
    )(swept, halo_up, halo_dn, mask_rows, cour)


def finish_kernel(rows, band_ref, delta_ref, out_ref, o_s):
    dests, cb, chunk = band_ref.shape
    lon = out_ref.shape[1]
    ways = lon // LANES
    for r in range(rows):
        for h in range(0, cb, 8):
            v = []
            for j in range(ways):
                d, at = divmod(r * lon + j * LANES, chunk)
                pick = (d, slice(h, h + 8), slice(at, at + LANES))
                v.append(band_ref[pick])
            w = []
            for j in range(ways):
                d, at = divmod(r * lon + j * LANES, chunk)
                w.append(delta_ref[d, :, at : at + LANES].astype(jnp.float32)[h : h + 8])
            back = gather_back([x + y for x, y in zip(v, w)])
            for j in range(ways):
                o_s[j, pl.ds(h * rows + r, 8, stride=rows), :] = back[j]
    for j in range(ways):
        out_ref[:, j * LANES : (j + 1) * LANES] = o_s[j]


def finish(band, delta, rows, lon):
    dests, comps, chunk = band.shape
    blk = pl.BlockSpec((dests, CB, chunk), lambda i: (0, i, 0))
    out = pl.pallas_call(
        functools.partial(finish_kernel, rows),
        grid=(pl.cdiv(comps, CB),),
        in_specs=[blk, blk],
        out_specs=pl.BlockSpec((CB * rows, lon), lambda i: (i, 0)),
        out_shape=jax.ShapeDtypeStruct((comps * rows, lon), jnp.float32),
        scratch_shapes=[pltpu.VMEM((lon // LANES, CB * rows, LANES), jnp.float32)],
        name="finish",
    )(band, delta)
    return out.reshape(comps, rows, lon)


NT = (((1,), (1,)), ((), ()))


def ocean_kernel(prof_ref, pts_ref, east_ref, north_ref, live_ref, vort_ref, diff_ref, out_ref, p_s, s_s):
    layers, points = prof_ref.shape
    slots = pts_ref.shape[0]
    per = LOW // layers
    for k in range(points // LOW):
        p_s[k * layers : (k + 1) * layers, :] = prof_ref[:, k * LOW : (k + 1) * LOW]
    lane = lax.broadcasted_iota(jnp.int32, (LOW, LOW), 1)
    block = lane // layers

    def pick(index, count, product):
        low = jnp.broadcast_to(index % LOW, (LOW, LOW))
        high = jnp.broadcast_to(index // LOW, (LOW, LOW)) - block
        hot = jnp.where(low == lane, 1.0, 0.0).astype(jnp.bfloat16)
        acc = jnp.zeros((LOW, LOW), jnp.float32)
        for m in range(-(-count // per)):
            acc = acc + jnp.where(high == m * per, product(hot, m), 0.0)
        return sum(acc[:, i * layers : (i + 1) * layers] for i in range(per))

    def from_points(hot, m):
        return lax.dot_general(hot, p_s[m * LOW : (m + 1) * LOW, :], NT, preferred_element_type=jnp.float32)

    s_s[...] = jnp.zeros_like(s_s)
    for j in range(slots // LOW):
        s = pick(pts_ref[j * LOW : (j + 1) * LOW, :], points // LOW, from_points)
        s_s[:, j * layers : (j + 1) * layers] = s.astype(jnp.bfloat16)

    def from_slots(hot, m):
        return jnp.dot(hot, s_s[:, m * LOW : (m + 1) * LOW], preferred_element_type=jnp.float32)

    for j in range(slots // LOW):
        rows = slice(j * LOW, (j + 1) * LOW)
        gap = pick(east_ref[rows, :], slots // LOW, from_slots) - pick(north_ref[rows, :], slots // LOW, from_slots)
        gap = gap.T
        s = s_s[:, j * layers : (j + 1) * layers].astype(jnp.float32).T
        upper = jnp.concatenate([s[:1], s[:-1]], axis=0)
        lower = jnp.concatenate([s[1:], jnp.zeros_like(s[:1])], axis=0)
        out_ref[:, rows] = live_ref[:, rows] * (
            vort_ref[:, rows] * gap + diff_ref[:, rows] * (upper - 2.0 * s + lower)
        )


def ocean(profile, pts, count, nbr, vort, diff):
    layers, points = profile.shape
    slots = pts.shape[0]
    per = LOW // layers
    lanes = -(-(slots // LOW) // per) * LOW
    live = (jnp.arange(slots, dtype=jnp.int32) < count).astype(jnp.float32)[None]
    return pl.pallas_call(
        ocean_kernel,
        out_shape=jax.ShapeDtypeStruct((layers, slots), jnp.float32),
        scratch_shapes=[
            pltpu.VMEM((points // LOW * layers, LOW), jnp.bfloat16),
            pltpu.VMEM((LOW, lanes), jnp.bfloat16),
        ],
        name="ocean",
    )(profile, pts[:, None], nbr[0][:, None], nbr[1][:, None], live, vort, diff)


def contract(weights, operand):
    return lax.dot_general(
        weights, operand, (((0,), (0,)), ((), ())), preferred_element_type=jnp.float32
    )


def on_device(
    spectrum,
    mask,
    courant,
    proj_a,
    proj_b,
    proj_c,
    proj_d,
    stokes_kernel,
    tile_points,
    tile_counts,
    tile_nbr,
    vorticity,
    diffusivity,
):
    comps, rows, lon = spectrum.shape
    margin = 2 * ADV
    bands, dests = lax.axis_size("lat"), lax.axis_size("comp")
    band_index = lax.axis_index("lat")
    sea = jnp.pad(mask.astype(jnp.float32), ((margin, margin), (0, 0)))
    ways = lon // LANES
    sea = sea.reshape(-1, LANES, ways).transpose(0, 2, 1).reshape(-1, lon)
    mask_rows = lax.dynamic_slice_in_dim(sea, band_index * rows, rows + 2 * margin, 0)
    up = [(i, i + 1) for i in range(bands - 1)]
    down = [(j, i) for i, j in up]

    def edge(part):
        return lax.optimization_barrier(part).astype(jnp.bfloat16).transpose(1, 0, 2)

    halo_up = lax.ppermute(edge(spectrum[:, rows - margin :]), "lat", up)
    halo_dn = lax.ppermute(edge(spectrum[:, :margin]), "lat", down)
    weights = [lax.all_gather(w, "comp", axis=0, tiled=True) for w in (proj_a, proj_b, proj_c, proj_d)]
    cour = courant.T
    swept = first_sweep(spectrum, mask_rows[margin : margin + rows], cour)
    bands_of, points_of = [], []
    width = pl.cdiv(pl.cdiv(comps, CB), PIECES) * CB
    for first in range(0, comps, width):
        piece = advect(
            swept, halo_up, halo_dn, mask_rows, cour, dests, first, min(width, comps - first)
        )
        bands_of.append(piece)
        points_of.append(lax.all_to_all(piece.astype(jnp.float16), "comp", split_axis=0, concat_axis=0))
    band = jnp.concatenate(bands_of, axis=1)
    points = jnp.concatenate(points_of, axis=1)
    chunk = points.shape[2]
    points = points.reshape(dests * comps, chunk)
    own = points.astype(jnp.float32)
    points = own.astype(jnp.bfloat16)
    product = (contract(weights[0], points) * contract(weights[1], points)).astype(jnp.bfloat16)
    delta = time_step * (contract(weights[2], product) - own * contract(weights[3], product))
    profile = lax.dot_general(
        stokes_kernel, own + delta, (((0,), (0,)), ((), ())), precision=lax.Precision.HIGHEST
    ).astype(jnp.bfloat16)
    group = lax.all_gather(profile, "comp", axis=1, tiled=True)
    back = lax.all_to_all(
        delta.astype(jnp.bfloat16).reshape(dests, comps, chunk), "comp", split_axis=0, concat_axis=0
    )
    where = tile_points[0, 0]
    cell = where % lon
    where = where - cell + cell % ways * LANES + cell // ways
    force = ocean(group, where, tile_counts[0, 0], tile_nbr[0, 0], vorticity[0, 0], diffusivity[0, 0])
    return finish(band, back, rows, lon), force[None, None]


def solution(mesh):
    return jax.shard_map(
        on_device,
        mesh=mesh,
        in_specs=(
            P("comp", "lat", None),
            P(),
            P(None, "comp"),
            P("comp", None),
            P("comp", None),
            P("comp", None),
            P("comp", None),
            P(),
            P("lat", "comp", None),
            P("lat", "comp"),
            P("lat", "comp", None, None),
            P("lat", "comp", None, None),
            P("lat", "comp", None, None),
        ),
        out_specs=(P("comp", "lat", None), P("lat", "comp", None, None)),
        check_vma=False,
    )
```

```python
import functools

import jax
import jax.numpy as jnp
from jax import lax
from jax.experimental import pallas as pl
from jax.experimental.pallas import tpu as pltpu
from jax.sharding import PartitionSpec as P

ADV = 2
time_step = 0.25
CB = 16
LANES = 128
LOW = 256
MESH = pl.DeviceIdType.MESH
STEPS = 16000.0


def half_limited(b, f):
    t = b * (1.0 / 6.0) + f * (1.0 / 3.0)
    low = jnp.minimum(jnp.maximum(b, f), 0.0)
    high = jnp.maximum(jnp.minimum(b, f), 0.0)
    return jnp.minimum(jnp.maximum(t, low), high)


def rolled(x, shift):
    return pltpu.roll(x, shift % LANES, 1)


def speeds(column, lon):
    c = jnp.broadcast_to(column, (8, lon))
    return c, jnp.abs(c), c > 0.0


def lon_row(e, sea, speed):
    c, a, pos = speed
    last = e.shape[1] - LANES
    nxt = jnp.concatenate([e[:, LANES:], rolled(e[:, :LANES], -1)], axis=1)
    d = nxt - e
    before = jnp.concatenate([rolled(d[:, last:], 1), d[:, :last]], axis=1)
    after = jnp.concatenate([d[:, LANES:], rolled(d[:, :LANES], -1)], axis=1)
    flux = c * jnp.where(pos, e, nxt) + a * half_limited(jnp.where(pos, before, after), d)
    behind = jnp.concatenate([rolled(flux[:, last:], 1), flux[:, :last]], axis=1)
    return sea * (e - (flux - behind))


def spreader(lon, back=False):
    ways = lon // LANES
    x = lax.broadcasted_iota(jnp.int32, (lon, lon), 1 if back else 0)
    at = lax.broadcasted_iota(jnp.int32, (lon, lon), 0 if back else 1)
    return (x == at % LANES * ways + at // LANES).astype(jnp.bfloat16)


def moved(x, ones):
    high = x.astype(jnp.bfloat16)
    low = (x - high.astype(jnp.float32)).astype(jnp.bfloat16)
    return jnp.dot(high, ones, preferred_element_type=jnp.float32) + jnp.dot(
        low, ones, preferred_element_type=jnp.float32
    )


def flipped(me, bit):
    return me + (1 - 2 * (me // (1 << bit) % 2)) * (1 << bit)


def advect_kernel(
    rows, dests, bands, x_ref, top_ref, end_ref, mask_ref, cour_ref, ones_ref, wa, wb, wc, wd,
    band_ref, pts_ref, ga, gb, gc, gd,
    x_s, swept_s, a_s, b_s, u_s, up_s, dn_s, send_s, own_s,
    halo_send, halo_recv, w_send, w_recv, p_send, p_recv, own_sem,
):
    lon = ones_ref.shape[0]
    chunk = rows * lon // dests
    ways = lon // LANES
    margin = 2 * ADV
    total = rows + 2 * margin
    comps = x_ref.shape[0] // rows
    blocks = comps // CB
    me, lat = lax.axis_index("comp"), lax.axis_index("lat")
    bits = dests.bit_length() - 1
    shards, gathered = (wa, wb, wc, wd), (ga, gb, gc, gd)

    barrier = pltpu.get_barrier_semaphore()
    for k in range(1, dests):
        pl.semaphore_signal(barrier, inc=1, device_id={"comp": (me + k) % dests}, device_id_type=MESH)

    @pl.when(lat + 1 < bands)
    def _():
        pl.semaphore_signal(barrier, inc=1, device_id={"lat": lat + 1}, device_id_type=MESH)

    @pl.when(lat > 0)
    def _():
        pl.semaphore_signal(barrier, inc=1, device_id={"lat": lat - 1}, device_id_type=MESH)

    beside = (lat + bands - 1) // bands + (2 * (bands - 1) - lat) // bands
    pl.semaphore_wait(barrier, dests - 1 + beside)

    def up_copy():
        return pltpu.make_async_remote_copy(
            src_ref=end_ref, dst_ref=up_s, send_sem=halo_send.at[0], recv_sem=halo_recv.at[0],
            device_id={"lat": lat + 1}, device_id_type=MESH,
        )

    def dn_copy():
        return pltpu.make_async_remote_copy(
            src_ref=top_ref, dst_ref=dn_s, send_sem=halo_send.at[1], recv_sem=halo_recv.at[1],
            device_id={"lat": lat - 1}, device_id_type=MESH,
        )

    @pl.when(lat + 1 < bands)
    def _():
        up_copy().start()

    @pl.when(lat > 0)
    def _():
        dn_copy().start()

    orders = [[*range(1, bits), 0], [*range(bits - 1, 0, -1), 0]]

    def weight_copies(m, phase):
        order = orders[m % 2]
        held = [me]
        for bit in order[:phase]:
            held = held + [flipped(h, bit) for h in held]
        to = flipped(me, order[phase])
        out = []
        for n, h in enumerate(held):
            at = (1 << phase) - 1 + n
            out.append(
                pltpu.make_async_remote_copy(
                    src_ref=shards[m] if n == 0 else gathered[m].at[h],
                    dst_ref=gathered[m].at[h],
                    send_sem=w_send.at[m, at],
                    recv_sem=w_recv.at[m, at],
                    device_id={"comp": to},
                    device_id_type=MESH,
                )
            )
        return out

    def weight_phase(phase):
        for m in range(4):
            if phase:
                for copy in weight_copies(m, phase - 1):
                    copy.wait_recv()
            if phase < bits:
                for copy in weight_copies(m, phase):
                    copy.start()

    weight_phase(0)
    loads = [pltpu.make_async_copy(shards[m], own_s.at[m], own_sem.at[m]) for m in range(4)]
    for copy in loads:
        copy.start()

    @pl.when(lat == 0)
    def _():
        up_s[...] = jnp.zeros_like(up_s)

    @pl.when(lat + 1 == bands)
    def _():
        dn_s[...] = jnp.zeros_like(dn_s)

    @pl.loop(0, blocks)
    def _(i):
        size = CB * rows
        whole = moved(x_ref[pl.ds(pl.multiple_of(i * size, size), size), :], ones_ref[...])
        for v in range(ways):
            x_s[v] = whole[:, v * LANES : (v + 1) * LANES]
        for half in range(CB // 8):
            base = pl.multiple_of(i * CB + half * 8, 8)
            speed = speeds(cour_ref[pl.ds(base, 8), 0:1], lon)
            for r in range(rows):
                sea = mask_ref[margin + r : margin + r + 1, :]
                first = half * (8 * rows) + r
                e = jnp.concatenate([x_s[v, pl.ds(first, 8, stride=rows), :] for v in range(ways)], axis=1)
                swept_s[r, pl.ds(base, 8), :] = lon_row(e * sea, sea, speed)

    stores = [pltpu.make_async_copy(own_s.at[m], gathered[m].at[me], own_sem.at[4 + m]) for m in range(4)]
    for m in range(4):
        loads[m].wait()
        stores[m].start()

    @pl.when(lat > 0)
    def _():
        up_copy().wait_recv()

    @pl.when(lat + 1 < bands)
    def _():
        dn_copy().wait_recv()

    if bits > 1:
        weight_phase(1)

    def point_copy(k, i):
        to = (me + k) % dests
        at = pl.ds(pl.multiple_of(i * CB, CB), CB)
        return pltpu.make_async_remote_copy(
            src_ref=send_s.at[to, at],
            dst_ref=pts_ref.at[me, at],
            send_sem=p_send.at[k - 1, i],
            recv_sem=p_recv.at[k - 1, i],
            device_id={"comp": to},
            device_id_type=MESH,
        )

    @pl.loop(0, blocks)
    def _(i):
        both = pl.ds(pl.multiple_of(i * CB, CB), CB)
        for k in range(2 * margin):
            src = up_s if k < margin else dn_s
            u_s[k] = jnp.dot(src[k % margin, both, :], ones_ref[...], preferred_element_type=jnp.float32)

        @pl.loop(0, CB // 8)
        def _(half):
            base = pl.multiple_of(i * CB + half * 8, 8)
            cour = cour_ref[pl.ds(base, 8), :]
            lon_speed = speeds(cour[:, 0:1], lon)
            c, a, pos = speeds(cour[:, 1:2], lon)

            def sea_row(r):
                return mask_ref[r : r + 1, :]

            def swept_row(r):
                if margin <= r < margin + rows:
                    return swept_s[r - margin, pl.ds(base, 8), :]
                return a_s[r]

            for k in range(2 * margin):
                r = k if k < margin else rows + k
                sea = sea_row(r)
                e = u_s[k, pl.ds(pl.multiple_of(half * 8, 8), 8), :] * sea
                a_s[r] = lon_row(e, sea, lon_speed)

            for substep in range(ADV):
                gone = 2 * substep
                row = swept_row
                if substep:
                    for r in range(gone, total - gone):
                        a_s[r] = lon_row(b_s[r], sea_row(r), lon_speed)
                    row = lambda r: a_s[r]
                cur, nxt, ahead = row(gone), row(gone + 1), row(gone + 2)
                d, dp, fl = nxt - cur, ahead - nxt, None
                for r in range(gone + 1, total - gone - 2):
                    cur, nxt, dm, d = nxt, ahead, d, dp
                    ahead = row(r + 2)
                    dp = ahead - nxt
                    now = c * jnp.where(pos, cur, nxt) + a * half_limited(jnp.where(pos, dm, dp), d)
                    if fl is not None:
                        value = sea_row(r) * (cur - (now - fl))
                        if substep == ADV - 1:
                            at = (r - margin) * lon
                            while at < (r - margin + 1) * lon:
                                to, lane = divmod(at, chunk)
                                n = min(chunk - lane, lon - at % lon)
                                band_ref[to, pl.ds(base, 8), lane : lane + n] = value[:, at % lon : at % lon + n]
                                at += n
                        else:
                            b_s[r] = value
                    fl = now

        for d in range(dests):
            value = band_ref[d, both, :] * STEPS + 0.5
            send_s[d, both, :] = value.astype(jnp.int32).astype(jnp.int16)
        for k in range(1, dests):
            point_copy(k, i).start()

    own_points = pltpu.make_async_copy(send_s.at[me], pts_ref.at[me], own_sem.at[8])
    own_points.start()
    for phase in range(2, bits + 1):
        weight_phase(phase)
    own_points.wait()
    for m in range(4):
        stores[m].wait()
        for phase in range(bits):
            for copy in weight_copies(m, phase):
                copy.wait_send()

    @pl.when(lat + 1 < bands)
    def _():
        up_copy().wait_send()

    @pl.when(lat > 0)
    def _():
        dn_copy().wait_send()

    @pl.loop(0, blocks)
    def _(i):
        for k in range(1, dests):
            point_copy(k, i).wait()


def advect(spectrum, top, end, mask_rows, cour, weights, dests, bands):
    comps, rows, lon = spectrum.shape
    chunk = rows * lon // dests
    margin = 2 * ADV
    total = rows + 2 * margin
    shard = weights[0].shape
    vmem = pl.BlockSpec(memory_space=pltpu.VMEM)
    hbm = pl.BlockSpec(memory_space=pl.ANY)
    copies = dests - 1
    dma = pltpu.SemaphoreType.DMA
    return pl.pallas_call(
        functools.partial(advect_kernel, rows, dests, bands),
        in_specs=[vmem] * 6 + [hbm] * 4,
        out_specs=[vmem] + [hbm] * 5,
        out_shape=[
            jax.ShapeDtypeStruct((dests, comps, chunk), jnp.float32),
            jax.ShapeDtypeStruct((dests, comps, chunk), jnp.int16),
        ]
        + [jax.ShapeDtypeStruct((dests, *shard), w.dtype) for w in weights],
        scratch_shapes=[
            pltpu.VMEM((lon // LANES, CB * rows, LANES), jnp.float32),
            pltpu.VMEM((rows, comps, lon), jnp.float32),
            pltpu.VMEM((total, 8, lon), jnp.float32),
            pltpu.VMEM((total, 8, lon), jnp.float32),
            pltpu.VMEM((2 * margin, CB, lon), jnp.float32),
            pltpu.VMEM((margin, comps, lon), jnp.bfloat16),
            pltpu.VMEM((margin, comps, lon), jnp.bfloat16),
            pltpu.VMEM((dests, comps, chunk), jnp.int16),
            pltpu.VMEM((4, *shard), jnp.bfloat16),
            dma((2,)),
            dma((2,)),
            dma((4, copies)),
            dma((4, copies)),
            dma((copies, comps // CB)),
            dma((copies, comps // CB)),
            dma((9,)),
        ],
        compiler_params=pltpu.CompilerParams(
            collective_id=0, has_side_effects=True, vmem_limit_bytes=60 * 1024 * 1024
        ),
        name="advect",
    )(spectrum.reshape(comps * rows, lon), top, end, mask_rows, cour, spreader(lon), *weights)


def finish_kernel(rows, band_ref, delta_ref, ones_ref, out_ref, f_s):
    dests, cb, chunk = band_ref.shape
    lon = out_ref.shape[1]
    for r in range(rows):
        at = 0
        while at < lon:
            d, lane = divmod(r * lon + at, chunk)
            n = min(chunk - lane, lon - at)
            v = band_ref[d, :, lane : lane + n] + delta_ref[d, :, lane : lane + n].astype(jnp.float32)
            for j in range(n // LANES):
                f_s[at // LANES + j, pl.ds(r, cb, stride=rows), :] = v[:, j * LANES : (j + 1) * LANES]
            at += n
    whole = jnp.concatenate([f_s[v] for v in range(lon // LANES)], axis=1)
    out_ref[...] = moved(whole, ones_ref[...])


def finish(band, delta, rows, lon):
    dests, comps, chunk = band.shape
    blk = pl.BlockSpec((dests, CB, chunk), lambda i: (0, i, 0))
    out = pl.pallas_call(
        functools.partial(finish_kernel, rows),
        grid=(pl.cdiv(comps, CB),),
        in_specs=[blk, blk, pl.BlockSpec((lon, lon), lambda i: (0, 0))],
        out_specs=pl.BlockSpec((CB * rows, lon), lambda i: (i, 0)),
        out_shape=jax.ShapeDtypeStruct((comps * rows, lon), jnp.float32),
        scratch_shapes=[pltpu.VMEM((lon // LANES, CB * rows, LANES), jnp.float32)],
        name="finish",
    )(band, delta, spreader(lon, back=True))
    return out.reshape(comps, rows, lon)


NT = (((1,), (1,)), ((), ()))


def ocean_kernel(prof_ref, pts_ref, east_ref, north_ref, live_ref, vort_ref, diff_ref, out_ref, p_s, s_s):
    layers, points = prof_ref.shape
    slots = pts_ref.shape[0]
    per = LOW // layers
    for k in range(points // LOW):
        p_s[k * layers : (k + 1) * layers, :] = prof_ref[:, k * LOW : (k + 1) * LOW]
    lane = lax.broadcasted_iota(jnp.int32, (LOW, LOW), 1)
    block = lane // layers

    def pick(index, count, product):
        low = jnp.broadcast_to(index % LOW, (LOW, LOW))
        high = jnp.broadcast_to(index // LOW, (LOW, LOW)) - block
        hot = jnp.where(low == lane, 1.0, 0.0).astype(jnp.bfloat16)
        acc = jnp.zeros((LOW, LOW), jnp.float32)
        for m in range(-(-count // per)):
            acc = acc + jnp.where(high == m * per, product(hot, m), 0.0)
        return sum(acc[:, i * layers : (i + 1) * layers] for i in range(per))

    def from_points(hot, m):
        return lax.dot_general(hot, p_s[m * LOW : (m + 1) * LOW, :], NT, preferred_element_type=jnp.float32)

    s_s[...] = jnp.zeros_like(s_s)
    for j in range(slots // LOW):
        s = pick(pts_ref[j * LOW : (j + 1) * LOW, :], points // LOW, from_points)
        s_s[:, j * layers : (j + 1) * layers] = s.astype(jnp.bfloat16)

    def from_slots(hot, m):
        return jnp.dot(hot, s_s[:, m * LOW : (m + 1) * LOW], preferred_element_type=jnp.float32)

    for j in range(slots // LOW):
        rows = slice(j * LOW, (j + 1) * LOW)
        gap = pick(east_ref[rows, :], slots // LOW, from_slots) - pick(north_ref[rows, :], slots // LOW, from_slots)
        gap = gap.T
        s = s_s[:, j * layers : (j + 1) * layers].astype(jnp.float32).T
        upper = jnp.concatenate([s[:1], s[:-1]], axis=0)
        lower = jnp.concatenate([s[1:], jnp.zeros_like(s[:1])], axis=0)
        out_ref[:, rows] = live_ref[:, rows] * (
            vort_ref[:, rows] * gap + diff_ref[:, rows] * (upper - 2.0 * s + lower)
        )


def ocean(profile, pts, count, nbr, vort, diff):
    layers, points = profile.shape
    slots = pts.shape[0]
    per = LOW // layers
    lanes = -(-(slots // LOW) // per) * LOW
    live = (jnp.arange(slots, dtype=jnp.int32) < count).astype(jnp.float32)[None]
    return pl.pallas_call(
        ocean_kernel,
        out_shape=jax.ShapeDtypeStruct((layers, slots), jnp.float32),
        scratch_shapes=[
            pltpu.VMEM((points // LOW * layers, LOW), jnp.bfloat16),
            pltpu.VMEM((LOW, lanes), jnp.bfloat16),
        ],
        name="ocean",
    )(profile, pts[:, None], nbr[0][:, None], nbr[1][:, None], live, vort, diff)


def contract(weights, operand):
    return lax.dot_general(
        weights, operand, (((0,), (0,)), ((), ())), preferred_element_type=jnp.float32
    )


def on_device(
    spectrum,
    mask,
    courant,
    proj_a,
    proj_b,
    proj_c,
    proj_d,
    stokes_kernel,
    tile_points,
    tile_counts,
    tile_nbr,
    vorticity,
    diffusivity,
):
    comps, rows, lon = spectrum.shape
    margin = 2 * ADV
    bands, dests = lax.axis_size("lat"), lax.axis_size("comp")
    band_index = lax.axis_index("lat")
    sea = jnp.pad(mask.astype(jnp.float32), ((margin, margin), (0, 0)))
    ways = lon // LANES
    sea = sea.reshape(-1, LANES, ways).transpose(0, 2, 1).reshape(-1, lon)
    mask_rows = lax.dynamic_slice_in_dim(sea, band_index * rows, rows + 2 * margin, 0)
    padded = pl.cdiv(comps, CB) * CB
    spread = ((0, padded - comps), (0, 0), (0, 0))
    top = spectrum[:, :margin].astype(jnp.bfloat16).transpose(1, 0, 2)
    end = spectrum[:, rows - margin :].astype(jnp.bfloat16).transpose(1, 0, 2)
    weights = (proj_a, proj_b, proj_c, proj_d)
    cour = courant.T
    start = spectrum
    if padded != comps:
        start = jnp.pad(spectrum, spread)
        cour = jnp.pad(cour, spread[:2])
        top, end = (jnp.pad(part, (spread[1], spread[0], spread[2])) for part in (top, end))
    band, points, *weights = advect(start, top, end, mask_rows, cour, weights, dests, bands)
    band, points = band[:, :comps], points[:, :comps]
    weights = [w.reshape(dests * comps, -1) for w in weights]
    chunk = points.shape[2]
    points = points.reshape(dests * comps, chunk)
    own = points.astype(jnp.float32) * (1.0 / STEPS)
    points = own.astype(jnp.bfloat16)
    product = (contract(weights[0], points) * contract(weights[1], points)).astype(jnp.bfloat16)
    delta = time_step * (contract(weights[2], product) - own * contract(weights[3], product))
    profile = lax.dot_general(
        stokes_kernel, own + delta, (((0,), (0,)), ((), ())), precision=lax.Precision.HIGHEST
    ).astype(jnp.bfloat16)
    group = lax.all_gather(profile, "comp", axis=1, tiled=True)
    back = lax.all_to_all(
        delta.astype(jnp.bfloat16).reshape(dests, comps, chunk), "comp", split_axis=0, concat_axis=0
    )
    where = tile_points[0, 0]
    cell = where % lon
    where = where - cell + cell % ways * LANES + cell // ways
    force = ocean(group, where, tile_counts[0, 0], tile_nbr[0, 0], vorticity[0, 0], diffusivity[0, 0])
    return finish(band, back, rows, lon), force[None, None]


def solution(mesh):
    return jax.shard_map(
        on_device,
        mesh=mesh,
        in_specs=(
            P("comp", "lat", None),
            P(),
            P(None, "comp"),
            P("comp", None),
            P("comp", None),
            P("comp", None),
            P("comp", None),
            P(),
            P("lat", "comp", None),
            P("lat", "comp"),
            P("lat", "comp", None, None),
            P("lat", "comp", None, None),
            P("lat", "comp", None, None),
        ),
        out_specs=(P("comp", "lat", None), P("lat", "comp", None, None)),
        check_vma=False,
    )
```

```python
import functools

import jax
import jax.numpy as jnp
from jax import lax
from jax.experimental import pallas as pl
from jax.experimental.pallas import tpu as pltpu
from jax.sharding import PartitionSpec as P

ADV = 2
time_step = 0.25
CB = 16
LANES = 128
LOW = 256
MESH = pl.DeviceIdType.MESH
STEPS = 16000.0


def half_limited(b, f):
    t = b * (1.0 / 6.0) + f * (1.0 / 3.0)
    low = jnp.minimum(jnp.maximum(b, f), 0.0)
    high = jnp.maximum(jnp.minimum(b, f), 0.0)
    return jnp.minimum(jnp.maximum(t, low), high)


def rolled(x, shift):
    return pltpu.roll(x, shift % LANES, 1)


def speeds(column, lon):
    c = jnp.broadcast_to(column, (8, lon))
    return c, jnp.abs(c), c > 0.0


def lon_row(e, sea, speed):
    c, a, pos = speed
    last = e.shape[1] - LANES
    nxt = jnp.concatenate([e[:, LANES:], rolled(e[:, :LANES], -1)], axis=1)
    d = nxt - e
    before = jnp.concatenate([rolled(d[:, last:], 1), d[:, :last]], axis=1)
    after = jnp.concatenate([d[:, LANES:], rolled(d[:, :LANES], -1)], axis=1)
    flux = c * jnp.where(pos, e, nxt) + a * half_limited(jnp.where(pos, before, after), d)
    behind = jnp.concatenate([rolled(flux[:, last:], 1), flux[:, :last]], axis=1)
    return sea * (e - (flux - behind))


def spreader(lon, back=False):
    ways = lon // LANES
    x = lax.broadcasted_iota(jnp.int32, (lon, lon), 1 if back else 0)
    at = lax.broadcasted_iota(jnp.int32, (lon, lon), 0 if back else 1)
    return (x == at % LANES * ways + at // LANES).astype(jnp.bfloat16)


def moved(x, ones):
    high = x.astype(jnp.bfloat16)
    low = (x - high.astype(jnp.float32)).astype(jnp.bfloat16)
    return jnp.dot(high, ones, preferred_element_type=jnp.float32) + jnp.dot(
        low, ones, preferred_element_type=jnp.float32
    )


def flipped(me, bit):
    return me + (1 - 2 * (me // (1 << bit) % 2)) * (1 << bit)


def advect_kernel(
    rows, dests, bands, x_ref, top_ref, end_ref, land_ref, cour_ref, ones_ref, wa, wb, wc, wd,
    band_ref, pts_ref, ga, gb, gc, gd,
    mask_ref, x_s, swept_s, a_s, b_s, u_s, up_s, dn_s, send_s, own_s,
    halo_send, halo_recv, w_send, w_recv, p_send, p_recv, own_sem,
):
    lon = ones_ref.shape[0]
    chunk = rows * lon // dests
    ways = lon // LANES
    margin = 2 * ADV
    total = rows + 2 * margin
    comps = x_ref.shape[0] // rows
    blocks = comps // CB
    me, lat = lax.axis_index("comp"), lax.axis_index("lat")
    bits = dests.bit_length() - 1
    shards, gathered = (wa, wb, wc, wd), (ga, gb, gc, gd)

    barrier = pltpu.get_barrier_semaphore()
    for k in range(1, dests):
        pl.semaphore_signal(barrier, inc=1, device_id={"comp": (me + k) % dests}, device_id_type=MESH)

    @pl.when(lat + 1 < bands)
    def _():
        pl.semaphore_signal(barrier, inc=1, device_id={"lat": lat + 1}, device_id_type=MESH)

    @pl.when(lat > 0)
    def _():
        pl.semaphore_signal(barrier, inc=1, device_id={"lat": lat - 1}, device_id_type=MESH)

    beside = (lat + bands - 1) // bands + (2 * (bands - 1) - lat) // bands
    pl.semaphore_wait(barrier, dests - 1 + beside)

    def up_copy():
        return pltpu.make_async_remote_copy(
            src_ref=end_ref, dst_ref=up_s, send_sem=halo_send.at[0], recv_sem=halo_recv.at[0],
            device_id={"lat": lat + 1}, device_id_type=MESH,
        )

    def dn_copy():
        return pltpu.make_async_remote_copy(
            src_ref=top_ref, dst_ref=dn_s, send_sem=halo_send.at[1], recv_sem=halo_recv.at[1],
            device_id={"lat": lat - 1}, device_id_type=MESH,
        )

    @pl.when(lat + 1 < bands)
    def _():
        up_copy().start()

    @pl.when(lat > 0)
    def _():
        dn_copy().start()

    orders = [[*range(1, bits), 0], [*range(bits - 1, 0, -1), 0]]

    def weight_copies(m, phase):
        order = orders[m % 2]
        held = [me]
        for bit in order[:phase]:
            held = held + [flipped(h, bit) for h in held]
        to = flipped(me, order[phase])
        out = []
        for n, h in enumerate(held):
            at = (1 << phase) - 1 + n
            out.append(
                pltpu.make_async_remote_copy(
                    src_ref=shards[m] if n == 0 else gathered[m].at[h],
                    dst_ref=gathered[m].at[h],
                    send_sem=w_send.at[m, at],
                    recv_sem=w_recv.at[m, at],
                    device_id={"comp": to},
                    device_id_type=MESH,
                )
            )
        return out

    def weight_phase(phase):
        for m in range(4):
            if phase:
                for copy in weight_copies(m, phase - 1):
                    copy.wait_recv()
            if phase < bits:
                for copy in weight_copies(m, phase):
                    copy.start()

    weight_phase(0)
    loads = [pltpu.make_async_copy(shards[m], own_s.at[m], own_sem.at[m]) for m in range(4)]
    for copy in loads:
        copy.start()

    @pl.when(lat == 0)
    def _():
        up_s[...] = jnp.zeros_like(up_s)

    @pl.when(lat + 1 == bands)
    def _():
        dn_s[...] = jnp.zeros_like(dn_s)

    mask_ref[...] = jnp.dot(land_ref[...].astype(jnp.bfloat16), ones_ref[...], preferred_element_type=jnp.float32)

    @pl.loop(0, blocks)
    def _(i):
        size = CB * rows
        whole = moved(x_ref[pl.ds(pl.multiple_of(i * size, size), size), :], ones_ref[...])
        for v in range(ways):
            x_s[v] = whole[:, v * LANES : (v + 1) * LANES]
        for half in range(CB // 8):
            base = pl.multiple_of(i * CB + half * 8, 8)
            speed = speeds(cour_ref[pl.ds(base, 8), 0:1], lon)
            for r in range(rows):
                sea = mask_ref[margin + r : margin + r + 1, :]
                first = half * (8 * rows) + r
                e = jnp.concatenate([x_s[v, pl.ds(first, 8, stride=rows), :] for v in range(ways)], axis=1)
                swept_s[r, pl.ds(base, 8), :] = lon_row(e * sea, sea, speed)

    stores = [pltpu.make_async_copy(own_s.at[m], gathered[m].at[me], own_sem.at[4 + m]) for m in range(4)]
    for m in range(4):
        loads[m].wait()
        stores[m].start()

    if bits > 1:
        weight_phase(1)

    @pl.when(lat > 0)
    def _():
        up_copy().wait_recv()

    @pl.when(lat + 1 < bands)
    def _():
        dn_copy().wait_recv()

    def point_copy(k, i):
        to = (me + k) % dests
        at = pl.ds(pl.multiple_of(i * CB, CB), CB)
        return pltpu.make_async_remote_copy(
            src_ref=send_s.at[to, at],
            dst_ref=pts_ref.at[me, at],
            send_sem=p_send.at[k - 1, i],
            recv_sem=p_recv.at[k - 1, i],
            device_id={"comp": to},
            device_id_type=MESH,
        )

    @pl.loop(0, blocks)
    def _(i):
        both = pl.ds(pl.multiple_of(i * CB, CB), CB)
        for k in range(2 * margin):
            src = up_s if k < margin else dn_s
            u_s[k] = jnp.dot(src[k % margin, both, :], ones_ref[...], preferred_element_type=jnp.float32)

        @pl.loop(0, CB // 8)
        def _(half):
            base = pl.multiple_of(i * CB + half * 8, 8)
            cour = cour_ref[pl.ds(base, 8), :]
            lon_speed = speeds(cour[:, 0:1], lon)
            c, a, pos = speeds(cour[:, 1:2], lon)

            def sea_row(r):
                return mask_ref[r : r + 1, :]

            def swept_row(r):
                if margin <= r < margin + rows:
                    return swept_s[r - margin, pl.ds(base, 8), :]
                return a_s[r]

            for k in range(2 * margin):
                r = k if k < margin else rows + k
                sea = sea_row(r)
                e = u_s[k, pl.ds(pl.multiple_of(half * 8, 8), 8), :] * sea
                a_s[r] = lon_row(e, sea, lon_speed)

            for substep in range(ADV):
                gone = 2 * substep
                row = swept_row
                if substep:
                    for r in range(gone, total - gone):
                        a_s[r] = lon_row(b_s[r], sea_row(r), lon_speed)
                    row = lambda r: a_s[r]
                cur, nxt, ahead = row(gone), row(gone + 1), row(gone + 2)
                d, dp, fl = nxt - cur, ahead - nxt, None
                for r in range(gone + 1, total - gone - 2):
                    cur, nxt, dm, d = nxt, ahead, d, dp
                    ahead = row(r + 2)
                    dp = ahead - nxt
                    now = c * jnp.where(pos, cur, nxt) + a * half_limited(jnp.where(pos, dm, dp), d)
                    if fl is not None:
                        value = sea_row(r) * (cur - (now - fl))
                        if substep == ADV - 1:
                            at = (r - margin) * lon
                            while at < (r - margin + 1) * lon:
                                to, lane = divmod(at, chunk)
                                n = min(chunk - lane, lon - at % lon)
                                band_ref[to, pl.ds(base, 8), lane : lane + n] = value[:, at % lon : at % lon + n]
                                at += n
                        else:
                            b_s[r] = value
                    fl = now

        for d in range(dests):
            value = band_ref[d, both, :] * STEPS + 0.5
            send_s[d, both, :] = value.astype(jnp.int32).astype(jnp.int16)
        for k in range(1, dests):
            point_copy(k, i).start()

    own_points = pltpu.make_async_copy(send_s.at[me], pts_ref.at[me], own_sem.at[8])
    own_points.start()
    for phase in range(2, bits + 1):
        weight_phase(phase)
    own_points.wait()
    for m in range(4):
        stores[m].wait()
        for phase in range(bits):
            for copy in weight_copies(m, phase):
                copy.wait_send()

    @pl.when(lat + 1 < bands)
    def _():
        up_copy().wait_send()

    @pl.when(lat > 0)
    def _():
        dn_copy().wait_send()

    @pl.loop(0, blocks)
    def _(i):
        for k in range(1, dests):
            point_copy(k, i).wait()


def advect(spectrum, top, end, mask_rows, cour, weights, dests, bands):
    comps, rows, lon = spectrum.shape
    chunk = rows * lon // dests
    margin = 2 * ADV
    total = rows + 2 * margin
    shard = weights[0].shape
    vmem = pl.BlockSpec(memory_space=pltpu.VMEM)
    hbm = pl.BlockSpec(memory_space=pl.ANY)
    copies = dests - 1
    dma = pltpu.SemaphoreType.DMA
    return pl.pallas_call(
        functools.partial(advect_kernel, rows, dests, bands),
        in_specs=[vmem] * 6 + [hbm] * 4,
        out_specs=[vmem] + [hbm] * 5,
        out_shape=[
            jax.ShapeDtypeStruct((dests, comps, chunk), jnp.float32),
            jax.ShapeDtypeStruct((dests, comps, chunk), jnp.int16),
        ]
        + [jax.ShapeDtypeStruct((dests, *shard), w.dtype) for w in weights],
        scratch_shapes=[
            pltpu.VMEM((total, lon), jnp.float32),
            pltpu.VMEM((lon // LANES, CB * rows, LANES), jnp.float32),
            pltpu.VMEM((rows, comps, lon), jnp.float32),
            pltpu.VMEM((total, 8, lon), jnp.float32),
            pltpu.VMEM((total, 8, lon), jnp.float32),
            pltpu.VMEM((2 * margin, CB, lon), jnp.float32),
            pltpu.VMEM((margin, comps, lon), jnp.bfloat16),
            pltpu.VMEM((margin, comps, lon), jnp.bfloat16),
            pltpu.VMEM((dests, comps, chunk), jnp.int16),
            pltpu.VMEM((4, *shard), jnp.bfloat16),
            dma((2,)),
            dma((2,)),
            dma((4, copies)),
            dma((4, copies)),
            dma((copies, comps // CB)),
            dma((copies, comps // CB)),
            dma((9,)),
        ],
        compiler_params=pltpu.CompilerParams(
            collective_id=0, has_side_effects=True, vmem_limit_bytes=60 * 1024 * 1024
        ),
        name="advect",
    )(spectrum.reshape(comps * rows, lon), top, end, mask_rows, cour, spreader(lon), *weights)


def finish_kernel(rows, band_ref, delta_ref, ones_ref, out_ref, f_s):
    dests, cb, chunk = band_ref.shape
    lon = out_ref.shape[1]
    for r in range(rows):
        at = 0
        while at < lon:
            d, lane = divmod(r * lon + at, chunk)
            n = min(chunk - lane, lon - at)
            v = band_ref[d, :, lane : lane + n] + delta_ref[d, :, lane : lane + n].astype(jnp.float32)
            for j in range(n // LANES):
                f_s[at // LANES + j, pl.ds(r, cb, stride=rows), :] = v[:, j * LANES : (j + 1) * LANES]
            at += n
    whole = jnp.concatenate([f_s[v] for v in range(lon // LANES)], axis=1)
    out_ref[...] = moved(whole, ones_ref[...])


def finish(band, delta, rows, lon):
    dests, comps, chunk = band.shape
    blk = pl.BlockSpec((dests, CB, chunk), lambda i: (0, i, 0))
    out = pl.pallas_call(
        functools.partial(finish_kernel, rows),
        grid=(pl.cdiv(comps, CB),),
        in_specs=[blk, blk, pl.BlockSpec((lon, lon), lambda i: (0, 0))],
        out_specs=pl.BlockSpec((CB * rows, lon), lambda i: (i, 0)),
        out_shape=jax.ShapeDtypeStruct((comps * rows, lon), jnp.float32),
        scratch_shapes=[pltpu.VMEM((lon // LANES, CB * rows, LANES), jnp.float32)],
        name="finish",
    )(band, delta, spreader(lon, back=True))
    return out.reshape(comps, rows, lon)


def ocean_kernel(lon, prof_ref, pts_ref, nbr_ref, count_ref, vort_ref, diff_ref, out_ref, g_s, p_s, s_s, send, recv):
    dests, layers, chunk = g_s.shape
    slots = pts_ref.shape[1]
    per = LOW // layers
    ways = lon // LANES
    me = lax.axis_index("comp")
    barrier = pltpu.get_barrier_semaphore()
    for k in range(1, dests):
        pl.semaphore_signal(barrier, inc=1, device_id={"comp": (me + k) % dests}, device_id_type=MESH)
    pl.semaphore_wait(barrier, dests - 1)
    copies = [
        pltpu.make_async_remote_copy(
            src_ref=prof_ref,
            dst_ref=g_s.at[me],
            send_sem=send.at[k - 1],
            recv_sem=recv.at[k - 1],
            device_id={"comp": (me + k) % dests},
            device_id_type=MESH,
        )
        for k in range(1, dests)
    ]
    for copy in copies:
        copy.start()
    g_s[me] = prof_ref[...]
    s_s[...] = jnp.zeros_like(s_s)
    row = lax.broadcasted_iota(jnp.int32, (LOW, LOW), 0)
    block = row // layers

    def pick(index, count, source):
        low = jnp.broadcast_to(index % LOW, (LOW, LOW))
        high = jnp.broadcast_to(index // LOW, (LOW, LOW)) - block
        hot = jnp.where(low == row, 1.0, 0.0).astype(jnp.bfloat16)
        acc = jnp.zeros((LOW, LOW), jnp.float32)
        for m in range(-(-count // per)):
            product = jnp.dot(source[m * LOW : (m + 1) * LOW, :], hot, preferred_element_type=jnp.float32)
            acc = acc + jnp.where(high == m * per, product, 0.0)
        return sum(acc[i * layers : (i + 1) * layers] for i in range(per))

    for copy in copies:
        copy.wait()
    for d in range(dests):
        for j in range(chunk // LOW):
            k = d * (chunk // LOW) + j
            p_s[k * layers : (k + 1) * layers, :] = g_s[d, :, j * LOW : (j + 1) * LOW]
    for j in range(slots // LOW):
        index = pts_ref[:, j * LOW : (j + 1) * LOW]
        cell = index % lon
        index = index - cell + cell % ways * LANES + cell // ways
        s = pick(index, dests * chunk // LOW, p_s)
        s_s[j * layers : (j + 1) * layers, :] = s.astype(jnp.bfloat16)
    lane = lax.broadcasted_iota(jnp.int32, (1, LOW), 1)
    for j in range(slots // LOW):
        part = slice(j * LOW, (j + 1) * LOW)
        gap = pick(nbr_ref[0:1, part], slots // LOW, s_s) - pick(nbr_ref[1:2, part], slots // LOW, s_s)
        s = s_s[j * layers : (j + 1) * layers, :].astype(jnp.float32)
        upper = jnp.concatenate([s[:1], s[:-1]], axis=0)
        lower = jnp.concatenate([s[1:], jnp.zeros_like(s[:1])], axis=0)
        live = jnp.where(lane + j * LOW < count_ref[...], 1.0, 0.0)
        out_ref[:, part] = live * (vort_ref[:, part] * gap + diff_ref[:, part] * (upper - 2.0 * s + lower))


def ocean(profile, pts, nbr, count, vort, diff, dests, lon):
    layers, chunk = profile.shape
    slots = pts.shape[1]
    per = LOW // layers
    depth = -(-(slots // LOW) // per) * LOW
    return pl.pallas_call(
        functools.partial(ocean_kernel, lon),
        out_shape=jax.ShapeDtypeStruct((layers, slots), jnp.float32),
        scratch_shapes=[
            pltpu.VMEM((dests, layers, chunk), profile.dtype),
            pltpu.VMEM((dests * chunk // LOW * layers, LOW), jnp.bfloat16),
            pltpu.VMEM((depth, LOW), jnp.bfloat16),
            pltpu.SemaphoreType.DMA((dests - 1,)),
            pltpu.SemaphoreType.DMA((dests - 1,)),
        ],
        compiler_params=pltpu.CompilerParams(collective_id=1, has_side_effects=True),
        name="ocean",
    )(profile, pts, nbr, count, vort, diff)


def contract(weights, operand):
    return lax.dot_general(
        weights, operand, (((0,), (0,)), ((), ())), preferred_element_type=jnp.float32
    )


def on_device(
    spectrum,
    mask,
    courant,
    proj_a,
    proj_b,
    proj_c,
    proj_d,
    stokes_kernel,
    tile_points,
    tile_counts,
    tile_nbr,
    vorticity,
    diffusivity,
):
    comps, rows, lon = spectrum.shape
    margin = 2 * ADV
    bands, dests = lax.axis_size("lat"), lax.axis_size("comp")
    band_index = lax.axis_index("lat")
    sea = jnp.pad(mask.astype(jnp.float32), ((margin, margin), (0, 0)))
    mask_rows = lax.dynamic_slice_in_dim(sea, band_index * rows, rows + 2 * margin, 0)
    padded = pl.cdiv(comps, CB) * CB
    spread = ((0, padded - comps), (0, 0), (0, 0))
    top, end = lax.optimization_barrier((spectrum[:, :margin], spectrum[:, rows - margin :]))
    top, end = (part.astype(jnp.bfloat16).transpose(1, 0, 2) for part in (top, end))
    weights = (proj_a, proj_b, proj_c, proj_d)
    cour = courant.T
    start = spectrum
    if padded != comps:
        start = jnp.pad(spectrum, spread)
        cour = jnp.pad(cour, spread[:2])
        top, end = (jnp.pad(part, (spread[1], spread[0], spread[2])) for part in (top, end))
    band, points, *weights = advect(start, top, end, mask_rows, cour, weights, dests, bands)
    band, points = band[:, :comps], points[:, :comps]
    weights = [w.reshape(dests * comps, -1) for w in weights]
    chunk = points.shape[2]
    points = points.reshape(dests * comps, chunk)
    own = points.astype(jnp.float32) * (1.0 / STEPS)
    points = own.astype(jnp.bfloat16)
    product = (contract(weights[0], points) * contract(weights[1], points)).astype(jnp.bfloat16)
    delta = time_step * (contract(weights[2], product) - own * contract(weights[3], product))
    profile = lax.dot_general(
        stokes_kernel, own + delta, (((0,), (0,)), ((), ())), precision=lax.Precision.HIGHEST
    ).astype(jnp.bfloat16)
    back = lax.all_to_all(
        delta.astype(jnp.bfloat16).reshape(dests, comps, chunk), "comp", split_axis=0, concat_axis=0
    )
    force = ocean(
        profile, tile_points[0], tile_nbr[0, 0], tile_counts, vorticity[0, 0], diffusivity[0, 0], dests, lon
    )
    return finish(band, back, rows, lon), force[None, None]


def solution(mesh):
    return jax.shard_map(
        on_device,
        mesh=mesh,
        in_specs=(
            P("comp", "lat", None),
            P(),
            P(None, "comp"),
            P("comp", None),
            P("comp", None),
            P("comp", None),
            P("comp", None),
            P(),
            P("lat", "comp", None),
            P("lat", "comp"),
            P("lat", "comp", None, None),
            P("lat", "comp", None, None),
            P("lat", "comp", None, None),
        ),
        out_specs=(P("comp", "lat", None), P("lat", "comp", None, None)),
        check_vma=False,
    )
```

```python
import functools

import jax
import jax.numpy as jnp
from jax import lax
from jax.experimental import pallas as pl
from jax.experimental.pallas import tpu as pltpu
from jax.sharding import PartitionSpec as P

ADV = 2
time_step = 0.25
CB = 16
LANES = 128
LOW = 256
MESH = pl.DeviceIdType.MESH
STEPS = 16000.0


def half_limited(b, f):
    t = b * (1.0 / 6.0) + f * (1.0 / 3.0)
    low = jnp.minimum(jnp.maximum(b, f), 0.0)
    high = jnp.maximum(jnp.minimum(b, f), 0.0)
    return jnp.minimum(jnp.maximum(t, low), high)


def rolled(x, shift):
    return pltpu.roll(x, shift % LANES, 1)


def speeds(column, lon):
    c = jnp.broadcast_to(column, (8, lon))
    return c, jnp.abs(c), c > 0.0


def lon_row(e, sea, speed):
    c, a, pos = speed
    last = e.shape[1] - LANES
    nxt = jnp.concatenate([e[:, LANES:], rolled(e[:, :LANES], -1)], axis=1)
    d = nxt - e
    before = jnp.concatenate([rolled(d[:, last:], 1), d[:, :last]], axis=1)
    after = jnp.concatenate([d[:, LANES:], rolled(d[:, :LANES], -1)], axis=1)
    flux = c * jnp.where(pos, e, nxt) + a * half_limited(jnp.where(pos, before, after), d)
    behind = jnp.concatenate([rolled(flux[:, last:], 1), flux[:, :last]], axis=1)
    return sea * (e - (flux - behind))


def spreader(lon, back=False):
    ways = lon // LANES
    x = lax.broadcasted_iota(jnp.int32, (lon, lon), 1 if back else 0)
    at = lax.broadcasted_iota(jnp.int32, (lon, lon), 0 if back else 1)
    return (x == at % LANES * ways + at // LANES).astype(jnp.bfloat16)


def moved(x, ones):
    high = x.astype(jnp.bfloat16)
    low = (x - high.astype(jnp.float32)).astype(jnp.bfloat16)
    return jnp.dot(high, ones, preferred_element_type=jnp.float32) + jnp.dot(
        low, ones, preferred_element_type=jnp.float32
    )


def flipped(me, bit):
    return me + (1 - 2 * (me // (1 << bit) % 2)) * (1 << bit)


def advect_kernel(
    rows, dests, bands, x_ref, land_ref, cour_ref, wa, wb, wc, wd,
    band_out, pts_ref, ga, gb, gc, gd,
    mask_ref, ones_ref, x_all, band_ref, x_s, swept_s, a_s, b_s, u_s, top_s, end_s, up_s, dn_s, send_s, own_s,
    halo_send, halo_recv, w_send, w_recv, p_send, p_recv, own_sem, band_sem, x_sem,
):
    lon = x_ref.shape[1]
    chunk = rows * lon // dests
    ways = lon // LANES
    margin = 2 * ADV
    total = rows + 2 * margin
    comps = x_ref.shape[0] // rows
    blocks = comps // CB
    me, lat = lax.axis_index("comp"), lax.axis_index("lat")
    bits = dests.bit_length() - 1
    shards, gathered = (wa, wb, wc, wd), (ga, gb, gc, gd)

    x_copy = pltpu.make_async_copy(x_ref, x_all, x_sem)
    x_copy.start()
    barrier = pltpu.get_barrier_semaphore()
    for k in range(1, dests):
        pl.semaphore_signal(barrier, inc=1, device_id={"comp": (me + k) % dests}, device_id_type=MESH)

    @pl.when(lat + 1 < bands)
    def _():
        pl.semaphore_signal(barrier, inc=1, device_id={"lat": lat + 1}, device_id_type=MESH)

    @pl.when(lat > 0)
    def _():
        pl.semaphore_signal(barrier, inc=1, device_id={"lat": lat - 1}, device_id_type=MESH)

    beside = (lat + bands - 1) // bands + (2 * (bands - 1) - lat) // bands
    pl.semaphore_wait(barrier, dests - 1 + beside)

    def block_at(i):
        return pl.ds(pl.multiple_of(i * CB, CB), CB)

    def up_copy(i):
        return pltpu.make_async_remote_copy(
            src_ref=end_s.at[:, block_at(i)], dst_ref=up_s.at[:, block_at(i)],
            send_sem=halo_send.at[0, i], recv_sem=halo_recv.at[0, i],
            device_id={"lat": lat + 1}, device_id_type=MESH,
        )

    def dn_copy(i):
        return pltpu.make_async_remote_copy(
            src_ref=top_s.at[:, block_at(i)], dst_ref=dn_s.at[:, block_at(i)],
            send_sem=halo_send.at[1, i], recv_sem=halo_recv.at[1, i],
            device_id={"lat": lat - 1}, device_id_type=MESH,
        )

    orders = [[*range(1, bits), 0], [*range(bits - 1, 0, -1), 0]]

    def weight_copies(m, phase):
        order = orders[m % 2]
        held = [me]
        for bit in order[:phase]:
            held = held + [flipped(h, bit) for h in held]
        to = flipped(me, order[phase])
        out = []
        for n, h in enumerate(held):
            at = (1 << phase) - 1 + n
            out.append(
                pltpu.make_async_remote_copy(
                    src_ref=shards[m] if n == 0 else gathered[m].at[h],
                    dst_ref=gathered[m].at[h],
                    send_sem=w_send.at[m, at],
                    recv_sem=w_recv.at[m, at],
                    device_id={"comp": to},
                    device_id_type=MESH,
                )
            )
        return out

    def weight_phase(phase):
        for m in range(4):
            if phase:
                for copy in weight_copies(m, phase - 1):
                    copy.wait_recv()
            if phase < bits:
                for copy in weight_copies(m, phase):
                    copy.start()

    weight_phase(0)
    loads = [pltpu.make_async_copy(shards[m], own_s.at[m], own_sem.at[m]) for m in range(4)]
    for copy in loads:
        copy.start()

    @pl.when(lat == 0)
    def _():
        up_s[...] = jnp.zeros_like(up_s)

    @pl.when(lat + 1 == bands)
    def _():
        dn_s[...] = jnp.zeros_like(dn_s)

    ones_ref[...] = spreader(lon)
    height = land_ref.shape[0]
    at_row = lax.broadcasted_iota(jnp.int32, (total, height), 0) + (lat * rows - margin)
    rows_of = (lax.broadcasted_iota(jnp.int32, (total, height), 1) == at_row).astype(jnp.bfloat16)
    land = land_ref[...].astype(jnp.float32).astype(jnp.bfloat16)
    land = jnp.dot(rows_of, land, preferred_element_type=jnp.float32).astype(jnp.bfloat16)
    mask_ref[...] = jnp.dot(land, ones_ref[...], preferred_element_type=jnp.float32)
    x_copy.wait()

    @pl.loop(0, blocks)
    def _(i):
        size = CB * rows
        whole = moved(x_all[pl.ds(pl.multiple_of(i * size, size), size), :], ones_ref[...])
        for v in range(ways):
            x_s[v] = whole[:, v * LANES : (v + 1) * LANES]
        halves = [pl.multiple_of(i * CB + h, 8) for h in range(0, CB, 8)]
        paces = [speeds(cour_ref[pl.ds(base, 8), 0:1], lon) for base in halves]
        for r in range(rows):
            sea = mask_ref[margin + r : margin + r + 1, :]
            lines = []
            for h, base in enumerate(halves):
                first = h * (8 * rows) + r
                e = jnp.concatenate([x_s[v, pl.ds(first, 8, stride=rows), :] for v in range(ways)], axis=1)
                lines.append(e)
                swept_s[r, pl.ds(base, 8), :] = lon_row(e * sea, sea, paces[h])
            if r < margin:
                top_s[r, block_at(i), :] = jnp.concatenate(lines, axis=0).astype(jnp.bfloat16)
            if r >= rows - margin:
                end_s[r - (rows - margin), block_at(i), :] = jnp.concatenate(lines, axis=0).astype(jnp.bfloat16)

        @pl.when(lat + 1 < bands)
        def _():
            up_copy(i).start()

        @pl.when(lat > 0)
        def _():
            dn_copy(i).start()

    stores = [pltpu.make_async_copy(own_s.at[m], gathered[m].at[me], own_sem.at[4 + m]) for m in range(4)]
    for m in range(4):
        loads[m].wait()
        stores[m].start()

    if bits > 1:
        weight_phase(1)

    def band_copy(i):
        return pltpu.make_async_copy(band_ref.at[:, block_at(i)], band_out.at[:, block_at(i)], band_sem.at[i])

    def point_copy(k, i):
        to = (me + k) % dests
        at = pl.ds(pl.multiple_of(i * CB, CB), CB)
        return pltpu.make_async_remote_copy(
            src_ref=send_s.at[to, at],
            dst_ref=pts_ref.at[me, at],
            send_sem=p_send.at[k - 1, i],
            recv_sem=p_recv.at[k - 1, i],
            device_id={"comp": to},
            device_id_type=MESH,
        )

    @pl.loop(0, blocks)
    def _(i):
        both = pl.ds(pl.multiple_of(i * CB, CB), CB)

        @pl.when(lat > 0)
        def _():
            up_copy(i).wait_recv()

        @pl.when(lat + 1 < bands)
        def _():
            dn_copy(i).wait_recv()

        for k in range(2 * margin):
            src = up_s if k < margin else dn_s
            u_s[k] = src[k % margin, both, :].astype(jnp.float32)

        @pl.loop(0, CB // 8)
        def _(half):
            base = pl.multiple_of(i * CB + half * 8, 8)
            cour = cour_ref[pl.ds(base, 8), :]
            lon_speed = speeds(cour[:, 0:1], lon)
            c, a, pos = speeds(cour[:, 1:2], lon)

            def sea_row(r):
                return mask_ref[r : r + 1, :]

            def swept_row(r):
                if margin <= r < margin + rows:
                    return swept_s[r - margin, pl.ds(base, 8), :]
                return a_s[r]

            for k in range(2 * margin):
                r = k if k < margin else rows + k
                sea = sea_row(r)
                e = u_s[k, pl.ds(pl.multiple_of(half * 8, 8), 8), :] * sea
                a_s[r] = lon_row(e, sea, lon_speed)

            for substep in range(ADV):
                gone = 2 * substep
                row = swept_row
                if substep:
                    for r in range(gone, total - gone):
                        a_s[r] = lon_row(b_s[r], sea_row(r), lon_speed)
                    row = lambda r: a_s[r]
                cur, nxt, ahead = row(gone), row(gone + 1), row(gone + 2)
                d, dp, fl = nxt - cur, ahead - nxt, None
                for r in range(gone + 1, total - gone - 2):
                    cur, nxt, dm, d = nxt, ahead, d, dp
                    ahead = row(r + 2)
                    dp = ahead - nxt
                    now = c * jnp.where(pos, cur, nxt) + a * half_limited(jnp.where(pos, dm, dp), d)
                    if fl is not None:
                        value = sea_row(r) * (cur - (now - fl))
                        if substep == ADV - 1:
                            at = (r - margin) * lon
                            while at < (r - margin + 1) * lon:
                                to, lane = divmod(at, chunk)
                                n = min(chunk - lane, lon - at % lon)
                                band_ref[to, pl.ds(base, 8), lane : lane + n] = value[:, at % lon : at % lon + n]
                                at += n
                        else:
                            b_s[r] = value
                    fl = now

        for d in range(dests):
            value = band_ref[d, both, :] * STEPS + 0.5
            send_s[d, both, :] = value.astype(jnp.int32).astype(jnp.int16)
        for k in range(1, dests):
            point_copy(k, i).start()
        band_copy(i).start()

    own_points = pltpu.make_async_copy(send_s.at[me], pts_ref.at[me], own_sem.at[8])
    own_points.start()
    for phase in range(2, bits + 1):
        weight_phase(phase)
    own_points.wait()
    for m in range(4):
        stores[m].wait()
        for phase in range(bits):
            for copy in weight_copies(m, phase):
                copy.wait_send()

    @pl.loop(0, blocks)
    def _(i):
        band_copy(i).wait()

        @pl.when(lat + 1 < bands)
        def _():
            up_copy(i).wait_send()

        @pl.when(lat > 0)
        def _():
            dn_copy(i).wait_send()

        for k in range(1, dests):
            point_copy(k, i).wait()


def advect(spectrum, mask, cour, weights, dests, bands):
    comps, rows, lon = spectrum.shape
    chunk = rows * lon // dests
    margin = 2 * ADV
    total = rows + 2 * margin
    shard = weights[0].shape
    vmem = pl.BlockSpec(memory_space=pltpu.VMEM)
    hbm = pl.BlockSpec(memory_space=pl.ANY)
    copies = dests - 1
    dma = pltpu.SemaphoreType.DMA
    return pl.pallas_call(
        functools.partial(advect_kernel, rows, dests, bands),
        in_specs=[hbm, vmem, vmem] + [hbm] * 4,
        out_specs=[hbm] * 6,
        out_shape=[
            jax.ShapeDtypeStruct((dests, comps, chunk), jnp.float32),
            jax.ShapeDtypeStruct((dests, comps, chunk), jnp.int16),
        ]
        + [jax.ShapeDtypeStruct((dests, *shard), w.dtype) for w in weights],
        scratch_shapes=[
            pltpu.VMEM((total, lon), jnp.float32),
            pltpu.VMEM((lon, lon), jnp.bfloat16),
            pltpu.VMEM((comps * rows, lon), jnp.float32),
            pltpu.VMEM((dests, comps, chunk), jnp.float32),
            pltpu.VMEM((lon // LANES, CB * rows, LANES), jnp.float32),
            pltpu.VMEM((rows, comps, lon), jnp.float32),
            pltpu.VMEM((total, 8, lon), jnp.float32),
            pltpu.VMEM((total, 8, lon), jnp.float32),
            pltpu.VMEM((2 * margin, CB, lon), jnp.float32),
            *[pltpu.VMEM((margin, comps, lon), jnp.bfloat16)] * 4,
            pltpu.VMEM((dests, comps, chunk), jnp.int16),
            pltpu.VMEM((4, *shard), jnp.bfloat16),
            dma((2, comps // CB)),
            dma((2, comps // CB)),
            dma((4, copies)),
            dma((4, copies)),
            dma((copies, comps // CB)),
            dma((copies, comps // CB)),
            dma((9,)),
            dma((comps // CB,)),
            dma(()),
        ],
        compiler_params=pltpu.CompilerParams(
            collective_id=0, has_side_effects=True, vmem_limit_bytes=60 * 1024 * 1024
        ),
        name="advect",
    )(spectrum.reshape(comps * rows, lon), mask, cour, *weights)


def finish_kernel(rows, band_ref, delta_ref, out_ref, ones_ref, f_s):
    dests, cb, chunk = band_ref.shape
    lon = out_ref.shape[1]

    @pl.when(pl.program_id(0) == 0)
    def _():
        ones_ref[...] = spreader(lon, back=True)

    for r in range(rows):
        at = 0
        while at < lon:
            d, lane = divmod(r * lon + at, chunk)
            n = min(chunk - lane, lon - at)
            v = band_ref[d, :, lane : lane + n] + delta_ref[d, :, lane : lane + n].astype(jnp.float32)
            for j in range(n // LANES):
                f_s[at // LANES + j, pl.ds(r, cb, stride=rows), :] = v[:, j * LANES : (j + 1) * LANES]
            at += n
    whole = jnp.concatenate([f_s[v] for v in range(lon // LANES)], axis=1)
    out_ref[...] = moved(whole, ones_ref[...])


def finish(band, delta, rows, lon):
    dests, comps, chunk = band.shape
    blk = pl.BlockSpec((dests, CB, chunk), lambda i: (0, i, 0))
    out = pl.pallas_call(
        functools.partial(finish_kernel, rows),
        grid=(pl.cdiv(comps, CB),),
        in_specs=[blk, blk],
        out_specs=pl.BlockSpec((CB * rows, lon), lambda i: (i, 0)),
        out_shape=jax.ShapeDtypeStruct((comps * rows, lon), jnp.float32),
        scratch_shapes=[
            pltpu.VMEM((lon, lon), jnp.bfloat16),
            pltpu.VMEM((lon // LANES, CB * rows, LANES), jnp.float32),
        ],
        name="finish",
    )(band, delta)
    return out.reshape(comps, rows, lon)


def ocean_kernel(
    lon, prof_ref, pts_ref, nbr_ref, count_ref, vort_ref, diff_ref, delta_ref, out_ref, back_ref,
    g_s, p_s, s_s, own_s, send, recv, far_send, far_recv, own_sem,
):
    dests, layers, chunk = g_s.shape
    slots = pts_ref.shape[1]
    per = LOW // layers
    ways = lon // LANES
    me = lax.axis_index("comp")
    barrier = pltpu.get_barrier_semaphore()
    for k in range(1, dests):
        pl.semaphore_signal(barrier, inc=1, device_id={"comp": (me + k) % dests}, device_id_type=MESH)
    pl.semaphore_wait(barrier, dests - 1)
    copies = [
        pltpu.make_async_remote_copy(
            src_ref=prof_ref,
            dst_ref=g_s.at[me],
            send_sem=send.at[k - 1],
            recv_sem=recv.at[k - 1],
            device_id={"comp": (me + k) % dests},
            device_id_type=MESH,
        )
        for k in range(1, dests)
    ]
    returns = [
        pltpu.make_async_remote_copy(
            src_ref=delta_ref.at[(me + k) % dests],
            dst_ref=back_ref.at[me],
            send_sem=far_send.at[k - 1],
            recv_sem=far_recv.at[k - 1],
            device_id={"comp": (me + k) % dests},
            device_id_type=MESH,
        )
        for k in range(1, dests)
    ]
    for copy in copies + returns:
        copy.start()
    load = pltpu.make_async_copy(delta_ref.at[me], own_s, own_sem.at[0])
    load.start()
    g_s[me] = prof_ref[...]
    s_s[...] = jnp.zeros_like(s_s)
    row = lax.broadcasted_iota(jnp.int32, (LOW, LOW), 0)
    block = row // layers

    def pick(index, count, source):
        low = jnp.broadcast_to(index % LOW, (LOW, LOW))
        high = jnp.broadcast_to(index // LOW, (LOW, LOW)) - block
        hot = jnp.where(low == row, 1.0, 0.0).astype(jnp.bfloat16)
        acc = jnp.zeros((LOW, LOW), jnp.float32)
        for m in range(-(-count // per)):
            product = jnp.dot(source[m * LOW : (m + 1) * LOW, :], hot, preferred_element_type=jnp.float32)
            acc = acc + jnp.where(high == m * per, product, 0.0)
        return sum(acc[i * layers : (i + 1) * layers] for i in range(per))

    load.wait()
    store = pltpu.make_async_copy(own_s, back_ref.at[me], own_sem.at[1])
    store.start()
    for copy in copies:
        copy.wait()
    for d in range(dests):
        for j in range(chunk // LOW):
            k = d * (chunk // LOW) + j
            p_s[k * layers : (k + 1) * layers, :] = g_s[d, :, j * LOW : (j + 1) * LOW]
    for j in range(slots // LOW):
        index = pts_ref[:, j * LOW : (j + 1) * LOW]
        cell = index % lon
        index = index - cell + cell % ways * LANES + cell // ways
        s = pick(index, dests * chunk // LOW, p_s)
        s_s[j * layers : (j + 1) * layers, :] = s.astype(jnp.bfloat16)
    lane = lax.broadcasted_iota(jnp.int32, (1, LOW), 1)
    for j in range(slots // LOW):
        part = slice(j * LOW, (j + 1) * LOW)
        gap = pick(nbr_ref[0:1, part], slots // LOW, s_s) - pick(nbr_ref[1:2, part], slots // LOW, s_s)
        s = s_s[j * layers : (j + 1) * layers, :].astype(jnp.float32)
        upper = jnp.concatenate([s[:1], s[:-1]], axis=0)
        lower = jnp.concatenate([s[1:], jnp.zeros_like(s[:1])], axis=0)
        live = jnp.where(lane + j * LOW < count_ref[...], 1.0, 0.0)
        out_ref[:, part] = live * (vort_ref[:, part] * gap + diff_ref[:, part] * (upper - 2.0 * s + lower))
    store.wait()
    for copy in returns:
        copy.wait()


def ocean(profile, pts, nbr, count, vort, diff, delta, lon):
    dests = delta.shape[0]
    layers, chunk = profile.shape
    slots = pts.shape[1]
    per = LOW // layers
    depth = -(-(slots // LOW) // per) * LOW
    return pl.pallas_call(
        functools.partial(ocean_kernel, lon),
        in_specs=[pl.BlockSpec(memory_space=pltpu.VMEM)] * 6 + [pl.BlockSpec(memory_space=pl.ANY)],
        out_specs=[pl.BlockSpec(memory_space=pltpu.VMEM), pl.BlockSpec(memory_space=pl.ANY)],
        out_shape=[
            jax.ShapeDtypeStruct((layers, slots), jnp.float32),
            jax.ShapeDtypeStruct(delta.shape, delta.dtype),
        ],
        scratch_shapes=[
            pltpu.VMEM((dests, layers, chunk), profile.dtype),
            pltpu.VMEM((dests * chunk // LOW * layers, LOW), jnp.bfloat16),
            pltpu.VMEM((depth, LOW), jnp.bfloat16),
            pltpu.VMEM(delta.shape[1:], delta.dtype),
            *[pltpu.SemaphoreType.DMA((dests - 1,))] * 4,
            pltpu.SemaphoreType.DMA((2,)),
        ],
        compiler_params=pltpu.CompilerParams(collective_id=1, has_side_effects=True),
        name="ocean",
    )(profile, pts, nbr, count, vort, diff, delta)


def contract(weights, operand):
    return lax.dot_general(
        weights, operand, (((0,), (0,)), ((), ())), preferred_element_type=jnp.float32
    )


def on_device(
    spectrum,
    mask,
    courant,
    proj_a,
    proj_b,
    proj_c,
    proj_d,
    stokes_kernel,
    tile_points,
    tile_counts,
    tile_nbr,
    vorticity,
    diffusivity,
):
    comps, rows, lon = spectrum.shape
    bands, dests = lax.axis_size("lat"), lax.axis_size("comp")
    padded = pl.cdiv(comps, CB) * CB
    spread = ((0, padded - comps), (0, 0), (0, 0))
    weights = (proj_a, proj_b, proj_c, proj_d)
    cour = courant.T
    start = spectrum
    if padded != comps:
        start = jnp.pad(spectrum, spread)
        cour = jnp.pad(cour, spread[:2])
    band, points, *weights = advect(start, mask, cour, weights, dests, bands)
    band, points = band[:, :comps], points[:, :comps]
    weights = [w.reshape(dests * comps, -1) for w in weights]
    chunk = points.shape[2]
    points = points.reshape(dests * comps, chunk)
    own = points.astype(jnp.float32) * (1.0 / STEPS)
    points = own.astype(jnp.bfloat16)
    product = (contract(weights[0], points) * contract(weights[1], points)).astype(jnp.bfloat16)
    delta = time_step * (contract(weights[2], product) - own * contract(weights[3], product))
    profile = lax.dot_general(
        stokes_kernel, own + delta, (((0,), (0,)), ((), ())), precision=lax.Precision.HIGHEST
    ).astype(jnp.bfloat16)
    force, back = ocean(
        profile, tile_points[0], tile_nbr[0, 0], tile_counts, vorticity[0, 0], diffusivity[0, 0],
        delta.astype(jnp.bfloat16).reshape(dests, comps, chunk), lon,
    )
    return finish(band, back, rows, lon), force[None, None]


def solution(mesh):
    return jax.shard_map(
        on_device,
        mesh=mesh,
        in_specs=(
            P("comp", "lat", None),
            P(),
            P(None, "comp"),
            P("comp", None),
            P("comp", None),
            P("comp", None),
            P("comp", None),
            P(),
            P("lat", "comp", None),
            P("lat", "comp"),
            P("lat", "comp", None, None),
            P("lat", "comp", None, None),
            P("lat", "comp", None, None),
        ),
        out_specs=(P("comp", "lat", None), P("lat", "comp", None, None)),
        check_vma=False,
    )
```

```python
import functools

import jax
import jax.numpy as jnp
from jax import lax
from jax.experimental import pallas as pl
from jax.experimental.pallas import tpu as pltpu
from jax.sharding import PartitionSpec as P

ADV = 2
time_step = 0.25
CB = 16
LANES = 128
LOW = 256
MESH = pl.DeviceIdType.MESH
STEPS = 16000.0


def half_limited(b, f):
    t = b * (1.0 / 6.0) + f * (1.0 / 3.0)
    low = jnp.minimum(jnp.maximum(b, f), 0.0)
    high = jnp.maximum(jnp.minimum(b, f), 0.0)
    return jnp.minimum(jnp.maximum(t, low), high)


def rolled(x, shift):
    return pltpu.roll(x, shift % LANES, 1)


def speeds(column, lon):
    c = jnp.broadcast_to(column, (8, lon))
    return c, jnp.abs(c), c > 0.0


def lon_row(e, sea, speed):
    c, a, pos = speed
    last = e.shape[1] - LANES
    nxt = jnp.concatenate([e[:, LANES:], rolled(e[:, :LANES], -1)], axis=1)
    d = nxt - e
    before = jnp.concatenate([rolled(d[:, last:], 1), d[:, :last]], axis=1)
    after = jnp.concatenate([d[:, LANES:], rolled(d[:, :LANES], -1)], axis=1)
    flux = c * jnp.where(pos, e, nxt) + a * half_limited(jnp.where(pos, before, after), d)
    behind = jnp.concatenate([rolled(flux[:, last:], 1), flux[:, :last]], axis=1)
    return sea * (e - (flux - behind))


def spreader(lon, back=False):
    ways = lon // LANES
    x = lax.broadcasted_iota(jnp.int32, (lon, lon), 1 if back else 0)
    at = lax.broadcasted_iota(jnp.int32, (lon, lon), 0 if back else 1)
    return (x == at % LANES * ways + at // LANES).astype(jnp.bfloat16)


def moved(x, ones):
    high = x.astype(jnp.bfloat16)
    low = (x - high.astype(jnp.float32)).astype(jnp.bfloat16)
    return jnp.dot(high, ones, preferred_element_type=jnp.float32) + jnp.dot(
        low, ones, preferred_element_type=jnp.float32
    )


def flipped(me, bit):
    return me + (1 - 2 * (me // (1 << bit) % 2)) * (1 << bit)


def advect_kernel(
    rows, dests, bands, x_ref, land_ref, cour_ref, wa, wb, wc, wd,
    band_out, pts_ref, ga, gb, gc, gd,
    mask_ref, ones_ref, x_all, band_ref, x_s, swept_s, a_s, b_s, u_s, top_s, end_s, up_s, dn_s, send_s, own_s,
    halo_send, halo_recv, w_send, w_recv, p_send, p_recv, own_sem, band_sem, x_sem,
):
    lon = x_ref.shape[1]
    chunk = rows * lon // dests
    ways = lon // LANES
    margin = 2 * ADV
    total = rows + 2 * margin
    comps = x_ref.shape[0] // rows
    blocks = comps // CB
    me, lat = lax.axis_index("comp"), lax.axis_index("lat")
    bits = dests.bit_length() - 1
    shards, gathered = (wa, wb, wc, wd), (ga, gb, gc, gd)

    x_copy = pltpu.make_async_copy(x_ref, x_all, x_sem)
    x_copy.start()
    barrier = pltpu.get_barrier_semaphore()
    for k in range(1, dests):
        pl.semaphore_signal(barrier, inc=1, device_id={"comp": (me + k) % dests}, device_id_type=MESH)

    @pl.when(lat + 1 < bands)
    def _():
        pl.semaphore_signal(barrier, inc=1, device_id={"lat": lat + 1}, device_id_type=MESH)

    @pl.when(lat > 0)
    def _():
        pl.semaphore_signal(barrier, inc=1, device_id={"lat": lat - 1}, device_id_type=MESH)

    beside = (lat + bands - 1) // bands + (2 * (bands - 1) - lat) // bands
    pl.semaphore_wait(barrier, dests - 1 + beside)

    def block_at(i):
        return pl.ds(pl.multiple_of(i * CB, CB), CB)

    def up_copy(i):
        return pltpu.make_async_remote_copy(
            src_ref=end_s.at[:, block_at(i)], dst_ref=up_s.at[:, block_at(i)],
            send_sem=halo_send.at[0, i], recv_sem=halo_recv.at[0, i],
            device_id={"lat": lat + 1}, device_id_type=MESH,
        )

    def dn_copy(i):
        return pltpu.make_async_remote_copy(
            src_ref=top_s.at[:, block_at(i)], dst_ref=dn_s.at[:, block_at(i)],
            send_sem=halo_send.at[1, i], recv_sem=halo_recv.at[1, i],
            device_id={"lat": lat - 1}, device_id_type=MESH,
        )

    orders = [[*range(1, bits), 0], [*range(bits - 1, 0, -1), 0]]

    def weight_copies(m, phase):
        order = orders[m % 2]
        held = [me]
        for bit in order[:phase]:
            held = held + [flipped(h, bit) for h in held]
        to = flipped(me, order[phase])
        out = []
        for n, h in enumerate(held):
            at = (1 << phase) - 1 + n
            out.append(
                pltpu.make_async_remote_copy(
                    src_ref=shards[m] if n == 0 else gathered[m].at[h],
                    dst_ref=gathered[m].at[h],
                    send_sem=w_send.at[m, at],
                    recv_sem=w_recv.at[m, at],
                    device_id={"comp": to},
                    device_id_type=MESH,
                )
            )
        return out

    def weight_phase(phase):
        for m in range(4):
            if phase:
                for copy in weight_copies(m, phase - 1):
                    copy.wait_recv()
            if phase < bits:
                for copy in weight_copies(m, phase):
                    copy.start()

    weight_phase(0)
    loads = [pltpu.make_async_copy(shards[m], own_s.at[m], own_sem.at[m]) for m in range(4)]
    for copy in loads:
        copy.start()

    @pl.when(lat == 0)
    def _():
        up_s[...] = jnp.zeros_like(up_s)

    @pl.when(lat + 1 == bands)
    def _():
        dn_s[...] = jnp.zeros_like(dn_s)

    ones_ref[...] = spreader(lon)
    height = land_ref.shape[0]
    at_row = lax.broadcasted_iota(jnp.int32, (total, height), 0) + (lat * rows - margin)
    rows_of = (lax.broadcasted_iota(jnp.int32, (total, height), 1) == at_row).astype(jnp.bfloat16)
    land = land_ref[...].astype(jnp.float32).astype(jnp.bfloat16)
    land = jnp.dot(rows_of, land, preferred_element_type=jnp.float32).astype(jnp.bfloat16)
    mask_ref[...] = jnp.dot(land, ones_ref[...], preferred_element_type=jnp.float32)
    x_copy.wait()

    @pl.loop(0, blocks)
    def _(i):
        size = CB * rows
        whole = moved(x_all[pl.ds(pl.multiple_of(i * size, size), size), :], ones_ref[...])
        for v in range(ways):
            x_s[v] = whole[:, v * LANES : (v + 1) * LANES]
        halves = [pl.multiple_of(i * CB + h, 8) for h in range(0, CB, 8)]
        paces = [speeds(cour_ref[pl.ds(base, 8), 0:1], lon) for base in halves]
        for r in range(rows):
            sea = mask_ref[margin + r : margin + r + 1, :]
            lines = []
            for h, base in enumerate(halves):
                first = h * (8 * rows) + r
                e = jnp.concatenate([x_s[v, pl.ds(first, 8, stride=rows), :] for v in range(ways)], axis=1)
                lines.append(e)
                swept_s[r, pl.ds(base, 8), :] = lon_row(e * sea, sea, paces[h])
            if r < margin:
                top_s[r, block_at(i), :] = jnp.concatenate(lines, axis=0).astype(jnp.bfloat16)
            if r >= rows - margin:
                end_s[r - (rows - margin), block_at(i), :] = jnp.concatenate(lines, axis=0).astype(jnp.bfloat16)

        @pl.when(lat + 1 < bands)
        def _():
            up_copy(i).start()

        @pl.when(lat > 0)
        def _():
            dn_copy(i).start()

    stores = [pltpu.make_async_copy(own_s.at[m], gathered[m].at[me], own_sem.at[4 + m]) for m in range(4)]
    for m in range(4):
        loads[m].wait()
        stores[m].start()

    if bits > 1:
        weight_phase(1)

    def band_copy(i):
        return pltpu.make_async_copy(band_ref.at[:, block_at(i)], band_out.at[:, block_at(i)], band_sem.at[i])

    def point_copy(k, i):
        to = (me + k) % dests
        at = pl.ds(pl.multiple_of(i * CB, CB), CB)
        return pltpu.make_async_remote_copy(
            src_ref=send_s.at[to, at],
            dst_ref=pts_ref.at[me, at],
            send_sem=p_send.at[k - 1, i],
            recv_sem=p_recv.at[k - 1, i],
            device_id={"comp": to},
            device_id_type=MESH,
        )

    @pl.loop(0, blocks)
    def _(i):
        both = pl.ds(pl.multiple_of(i * CB, CB), CB)

        @pl.when(lat > 0)
        def _():
            up_copy(i).wait_recv()

        @pl.when(lat + 1 < bands)
        def _():
            dn_copy(i).wait_recv()

        for k in range(2 * margin):
            src = up_s if k < margin else dn_s
            u_s[k] = src[k % margin, both, :].astype(jnp.float32)

        @pl.loop(0, CB // 8)
        def _(half):
            base = pl.multiple_of(i * CB + half * 8, 8)
            cour = cour_ref[pl.ds(base, 8), :]
            lon_speed = speeds(cour[:, 0:1], lon)
            c, a, pos = speeds(cour[:, 1:2], lon)

            def sea_row(r):
                return mask_ref[r : r + 1, :]

            def swept_row(r):
                if margin <= r < margin + rows:
                    return swept_s[r - margin, pl.ds(base, 8), :]
                return a_s[r]

            for k in range(2 * margin):
                r = k if k < margin else rows + k
                sea = sea_row(r)
                e = u_s[k, pl.ds(pl.multiple_of(half * 8, 8), 8), :] * sea
                a_s[r] = lon_row(e, sea, lon_speed)

            for substep in range(ADV):
                gone = 2 * substep
                row = swept_row
                if substep:
                    for r in range(gone, total - gone):
                        a_s[r] = lon_row(b_s[r], sea_row(r), lon_speed)
                    row = lambda r: a_s[r]
                cur, nxt, ahead = row(gone), row(gone + 1), row(gone + 2)
                d, dp, fl = nxt - cur, ahead - nxt, None
                for r in range(gone + 1, total - gone - 2):
                    cur, nxt, dm, d = nxt, ahead, d, dp
                    ahead = row(r + 2)
                    dp = ahead - nxt
                    now = c * jnp.where(pos, cur, nxt) + a * half_limited(jnp.where(pos, dm, dp), d)
                    if fl is not None:
                        value = sea_row(r) * (cur - (now - fl))
                        if substep == ADV - 1:
                            at = (r - margin) * lon
                            while at < (r - margin + 1) * lon:
                                to, lane = divmod(at, chunk)
                                n = min(chunk - lane, lon - at % lon)
                                band_ref[to, pl.ds(base, 8), lane : lane + n] = value[:, at % lon : at % lon + n]
                                at += n
                        else:
                            b_s[r] = value
                    fl = now

        for d in range(dests):
            value = band_ref[d, both, :] * STEPS + 0.5
            send_s[d, both, :] = value.astype(jnp.int32).astype(jnp.int16)
        for k in range(1, dests):
            point_copy(k, i).start()
        band_copy(i).start()

    own_points = pltpu.make_async_copy(send_s.at[me], pts_ref.at[me], own_sem.at[8])
    own_points.start()
    for phase in range(2, bits + 1):
        weight_phase(phase)
    own_points.wait()
    for m in range(4):
        stores[m].wait()
        for phase in range(bits):
            for copy in weight_copies(m, phase):
                copy.wait_send()

    @pl.loop(0, blocks)
    def _(i):
        band_copy(i).wait()

        @pl.when(lat + 1 < bands)
        def _():
            up_copy(i).wait_send()

        @pl.when(lat > 0)
        def _():
            dn_copy(i).wait_send()

        for k in range(1, dests):
            point_copy(k, i).wait()


def advect(spectrum, mask, cour, weights, dests, bands):
    comps, rows, lon = spectrum.shape
    chunk = rows * lon // dests
    margin = 2 * ADV
    total = rows + 2 * margin
    shard = weights[0].shape
    vmem = pl.BlockSpec(memory_space=pltpu.VMEM)
    hbm = pl.BlockSpec(memory_space=pl.ANY)
    copies = dests - 1
    dma = pltpu.SemaphoreType.DMA
    return pl.pallas_call(
        functools.partial(advect_kernel, rows, dests, bands),
        in_specs=[hbm, vmem, vmem] + [hbm] * 4,
        out_specs=[hbm] * 6,
        out_shape=[
            jax.ShapeDtypeStruct((dests, comps, chunk), jnp.float32),
            jax.ShapeDtypeStruct((dests, comps, chunk), jnp.int16),
        ]
        + [jax.ShapeDtypeStruct((dests, *shard), w.dtype) for w in weights],
        scratch_shapes=[
            pltpu.VMEM((total, lon), jnp.float32),
            pltpu.VMEM((lon, lon), jnp.bfloat16),
            pltpu.VMEM((comps * rows, lon), jnp.float32),
            pltpu.VMEM((dests, comps, chunk), jnp.float32),
            pltpu.VMEM((lon // LANES, CB * rows, LANES), jnp.float32),
            pltpu.VMEM((rows, comps, lon), jnp.float32),
            pltpu.VMEM((total, 8, lon), jnp.float32),
            pltpu.VMEM((total, 8, lon), jnp.float32),
            pltpu.VMEM((2 * margin, CB, lon), jnp.float32),
            *[pltpu.VMEM((margin, comps, lon), jnp.bfloat16)] * 4,
            pltpu.VMEM((dests, comps, chunk), jnp.int16),
            pltpu.VMEM((4, *shard), jnp.bfloat16),
            dma((2, comps // CB)),
            dma((2, comps // CB)),
            dma((4, copies)),
            dma((4, copies)),
            dma((copies, comps // CB)),
            dma((copies, comps // CB)),
            dma((9,)),
            dma((comps // CB,)),
            dma(()),
        ],
        compiler_params=pltpu.CompilerParams(
            collective_id=0, has_side_effects=True, vmem_limit_bytes=60 * 1024 * 1024
        ),
        name="advect",
    )(spectrum.reshape(comps * rows, lon), mask, cour, *weights)


def lay_rows(rows, lon, part, f_s):
    dests, cb, chunk = part.shape
    for r in range(rows):
        at = 0
        while at < lon:
            d, lane = divmod(r * lon + at, chunk)
            n = min(chunk - lane, lon - at)
            v = part[d, :, lane : lane + n].astype(jnp.float32)
            for j in range(n // LANES):
                f_s[at // LANES + j, pl.ds(r, cb, stride=rows), :] = v[:, j * LANES : (j + 1) * LANES]
            at += n
    return jnp.concatenate([f_s[v] for v in range(lon // LANES)], axis=1)


def finish_kernel(rows, band_ref, delta_ref, out_ref, ones_ref, f_s):
    @pl.when(pl.program_id(0) == 0)
    def _():
        ones_ref[...] = spreader(out_ref.shape[1], back=True)

    whole = lay_rows(rows, out_ref.shape[1], delta_ref, f_s).astype(jnp.bfloat16)
    out_ref[...] = band_ref[...] + jnp.dot(whole, ones_ref[...], preferred_element_type=jnp.float32)


def finish(band, delta, rows):
    dests, comps, chunk = delta.shape
    lon = band.shape[1]
    line = pl.BlockSpec((CB * rows, lon), lambda i: (i, 0))
    out = pl.pallas_call(
        functools.partial(finish_kernel, rows),
        grid=(pl.cdiv(comps, CB),),
        in_specs=[line, pl.BlockSpec((dests, CB, chunk), lambda i: (0, i, 0))],
        out_specs=line,
        out_shape=jax.ShapeDtypeStruct((comps * rows, lon), jnp.float32),
        scratch_shapes=[
            pltpu.VMEM((lon, lon), jnp.bfloat16),
            pltpu.VMEM((lon // LANES, CB * rows, LANES), jnp.float32),
        ],
        name="finish",
    )(band, delta)
    return out.reshape(comps, rows, lon)


def ocean_kernel(
    lon, prof_ref, pts_ref, nbr_ref, count_ref, vort_ref, diff_ref, delta_ref, band_ref, out_ref, back_ref, line_ref,
    g_s, p_s, s_s, own_s, band_s, line_s, f_s, ones_s, send, recv, far_send, far_recv, own_sem, line_sem,
):
    dests, layers, chunk = g_s.shape
    slots = pts_ref.shape[1]
    per = LOW // layers
    ways = lon // LANES
    rows = dests * chunk // lon
    blocks = band_s.shape[1] // CB
    me = lax.axis_index("comp")
    band_load = pltpu.make_async_copy(band_ref, band_s, own_sem.at[2])
    band_load.start()
    barrier = pltpu.get_barrier_semaphore()
    for k in range(1, dests):
        pl.semaphore_signal(barrier, inc=1, device_id={"comp": (me + k) % dests}, device_id_type=MESH)
    pl.semaphore_wait(barrier, dests - 1)
    copies = [
        pltpu.make_async_remote_copy(
            src_ref=prof_ref,
            dst_ref=g_s.at[me],
            send_sem=send.at[k - 1],
            recv_sem=recv.at[k - 1],
            device_id={"comp": (me + k) % dests},
            device_id_type=MESH,
        )
        for k in range(1, dests)
    ]
    returns = [
        pltpu.make_async_remote_copy(
            src_ref=delta_ref.at[(me + k) % dests],
            dst_ref=back_ref.at[me],
            send_sem=far_send.at[k - 1],
            recv_sem=far_recv.at[k - 1],
            device_id={"comp": (me + k) % dests},
            device_id_type=MESH,
        )
        for k in range(1, dests)
    ]
    for copy in copies + returns:
        copy.start()
    load = pltpu.make_async_copy(delta_ref.at[me], own_s, own_sem.at[0])
    load.start()
    g_s[me] = prof_ref[...]
    s_s[...] = jnp.zeros_like(s_s)
    row = lax.broadcasted_iota(jnp.int32, (LOW, LOW), 0)
    block = row // layers

    def pick(index, count, source):
        low = jnp.broadcast_to(index % LOW, (LOW, LOW))
        high = jnp.broadcast_to(index // LOW, (LOW, LOW)) - block
        hot = jnp.where(low == row, 1.0, 0.0).astype(jnp.bfloat16)
        acc = jnp.zeros((LOW, LOW), jnp.float32)
        for m in range(-(-count // per)):
            product = jnp.dot(source[m * LOW : (m + 1) * LOW, :], hot, preferred_element_type=jnp.float32)
            acc = acc + jnp.where(high == m * per, product, 0.0)
        return sum(acc[i * layers : (i + 1) * layers] for i in range(per))

    load.wait()
    store = pltpu.make_async_copy(own_s, back_ref.at[me], own_sem.at[1])
    store.start()
    for copy in copies:
        copy.wait()
    for d in range(dests):
        for j in range(chunk // LOW):
            k = d * (chunk // LOW) + j
            p_s[k * layers : (k + 1) * layers, :] = g_s[d, :, j * LOW : (j + 1) * LOW]
    for j in range(slots // LOW):
        index = pts_ref[:, j * LOW : (j + 1) * LOW]
        cell = index % lon
        index = index - cell + cell % ways * LANES + cell // ways
        s = pick(index, dests * chunk // LOW, p_s)
        s_s[j * layers : (j + 1) * layers, :] = s.astype(jnp.bfloat16)
    lane = lax.broadcasted_iota(jnp.int32, (1, LOW), 1)
    for j in range(slots // LOW):
        part = slice(j * LOW, (j + 1) * LOW)
        gap = pick(nbr_ref[0:1, part], slots // LOW, s_s) - pick(nbr_ref[1:2, part], slots // LOW, s_s)
        s = s_s[j * layers : (j + 1) * layers, :].astype(jnp.float32)
        upper = jnp.concatenate([s[:1], s[:-1]], axis=0)
        lower = jnp.concatenate([s[1:], jnp.zeros_like(s[:1])], axis=0)
        live = jnp.where(lane + j * LOW < count_ref[...], 1.0, 0.0)
        out_ref[:, part] = live * (vort_ref[:, part] * gap + diff_ref[:, part] * (upper - 2.0 * s + lower))
    band_load.wait()
    ones_s[...] = spreader(lon, back=True)

    def line_copy(i):
        at = pl.ds(pl.multiple_of(i * (CB * rows), CB * rows), CB * rows)
        return pltpu.make_async_copy(line_s.at[at], line_ref.at[at], line_sem.at[i])

    @pl.loop(0, blocks)
    def _(i):
        part = band_s.at[:, pl.ds(pl.multiple_of(i * CB, CB), CB)]
        at = pl.ds(pl.multiple_of(i * (CB * rows), CB * rows), CB * rows)
        line_s[at, :] = moved(lay_rows(rows, lon, part, f_s), ones_s[...])
        line_copy(i).start()

    store.wait()
    for copy in returns:
        copy.wait()

    @pl.loop(0, blocks)
    def _(i):
        line_copy(i).wait()


def ocean(profile, pts, nbr, count, vort, diff, delta, band, lon):
    dests = delta.shape[0]
    comps = band.shape[1]
    rows = dests * band.shape[2] // lon
    layers, chunk = profile.shape
    slots = pts.shape[1]
    per = LOW // layers
    depth = -(-(slots // LOW) // per) * LOW
    return pl.pallas_call(
        functools.partial(ocean_kernel, lon),
        in_specs=[pl.BlockSpec(memory_space=pltpu.VMEM)] * 6 + [pl.BlockSpec(memory_space=pl.ANY)] * 2,
        out_specs=[pl.BlockSpec(memory_space=pltpu.VMEM)] + [pl.BlockSpec(memory_space=pl.ANY)] * 2,
        out_shape=[
            jax.ShapeDtypeStruct((layers, slots), jnp.float32),
            jax.ShapeDtypeStruct(delta.shape, delta.dtype),
            jax.ShapeDtypeStruct((comps * rows, lon), jnp.float32),
        ],
        scratch_shapes=[
            pltpu.VMEM((dests, layers, chunk), profile.dtype),
            pltpu.VMEM((dests * chunk // LOW * layers, LOW), jnp.bfloat16),
            pltpu.VMEM((depth, LOW), jnp.bfloat16),
            pltpu.VMEM(delta.shape[1:], delta.dtype),
            pltpu.VMEM(band.shape, jnp.float32),
            pltpu.VMEM((comps * rows, lon), jnp.float32),
            pltpu.VMEM((lon // LANES, CB * rows, LANES), jnp.float32),
            pltpu.VMEM((lon, lon), jnp.bfloat16),
            *[pltpu.SemaphoreType.DMA((dests - 1,))] * 4,
            pltpu.SemaphoreType.DMA((3,)),
            pltpu.SemaphoreType.DMA((comps // CB,)),
        ],
        compiler_params=pltpu.CompilerParams(collective_id=1, has_side_effects=True),
        name="ocean",
    )(profile, pts, nbr, count, vort, diff, delta, band)


def contract(weights, operand):
    return lax.dot_general(
        weights, operand, (((0,), (0,)), ((), ())), preferred_element_type=jnp.float32
    )


def on_device(
    spectrum,
    mask,
    courant,
    proj_a,
    proj_b,
    proj_c,
    proj_d,
    stokes_kernel,
    tile_points,
    tile_counts,
    tile_nbr,
    vorticity,
    diffusivity,
):
    comps, rows, lon = spectrum.shape
    bands, dests = lax.axis_size("lat"), lax.axis_size("comp")
    padded = pl.cdiv(comps, CB) * CB
    spread = ((0, padded - comps), (0, 0), (0, 0))
    weights = (proj_a, proj_b, proj_c, proj_d)
    cour = courant.T
    start = spectrum
    if padded != comps:
        start = jnp.pad(spectrum, spread)
        cour = jnp.pad(cour, spread[:2])
    band, points, *weights = advect(start, mask, cour, weights, dests, bands)
    points = points[:, :comps]
    weights = [w.reshape(dests * comps, -1) for w in weights]
    chunk = points.shape[2]
    points = points.reshape(dests * comps, chunk)
    own = points.astype(jnp.float32) * (1.0 / STEPS)
    points = own.astype(jnp.bfloat16)
    product = (contract(weights[0], points) * contract(weights[1], points)).astype(jnp.bfloat16)
    delta = time_step * (contract(weights[2], product) - own * contract(weights[3], product))
    profile = lax.dot_general(
        stokes_kernel, own + delta, (((0,), (0,)), ((), ())), precision=lax.Precision.HIGHEST
    ).astype(jnp.bfloat16)
    force, back, lines = ocean(
        profile, tile_points[0], tile_nbr[0, 0], tile_counts, vorticity[0, 0], diffusivity[0, 0],
        delta.astype(jnp.bfloat16).reshape(dests, comps, chunk), band, lon,
    )
    return finish(lines, back, rows), force[None, None]


def solution(mesh):
    return jax.shard_map(
        on_device,
        mesh=mesh,
        in_specs=(
            P("comp", "lat", None),
            P(),
            P(None, "comp"),
            P("comp", None),
            P("comp", None),
            P("comp", None),
            P("comp", None),
            P(),
            P("lat", "comp", None),
            P("lat", "comp"),
            P("lat", "comp", None, None),
            P("lat", "comp", None, None),
            P("lat", "comp", None, None),
        ),
        out_specs=(P("comp", "lat", None), P("lat", "comp", None, None)),
        check_vma=False,
    )
```
